256 devices in a mesh: row: 16 (over y, z_hi), col: 16 (over x, z_lo, core).
Axes of the slice: x: 4, y: 4, z: 8 (z_hi: 4, z_lo: 2; z = z_hi * 2 + z_lo), core: 2. Of those that a mesh axis runs over, the one named last changes fastest.
Arguments:
- image: bfloat16 [512, 512, 192], P('row', 'col'), may hold values from -6 to 6
- conv_weight: bfloat16 [3, 3, 192, 384], replicated, may hold values from -0.15625 to 0.15625
- conv_bias: float32 [384], replicated, may hold values from -3 to 3
- merge_gain: float32 [384], replicated, may hold values from 0.25 to 1.75
- merge_shift: float32 [384], replicated, may hold values from -3 to 3
- norm_gain: float32 [384], replicated, may hold values from 0.25 to 1.75
- norm_shift: float32 [384], replicated, may hold values from -3 to 3
- qkv_weight: bfloat16 [384, 1152], replicated, may hold values from -4 to 4
- proj_weight: bfloat16 [384, 384], replicated, may hold values from -0.3125 to 0.3125
- proj_bias: float32 [384], replicated, may hold values from -3 to 3
Outputs:
- block_out: bfloat16 [256, 256, 384], P('row', 'col')
The draws below stay inside these ranges and needn't reach their ends.
All inputs are finite; a program needn't handle non-finite values.
Results may differ from the reference program's by a relative error of at most 0.02.
The reference program's roundings to bfloat16 on the way (of `tokens`, `normed`, `qkv`, `probs` and `attention`) count: a program that leaves them out, or rounds other values in their place, can miss the bound.
Values may be sent and summed in bfloat16 or wider, within the bound.
A program may use at most 128 MiB of HBM per device.

```python
import math
import jax
import jax.numpy as jnp
from jax import lax

IN_CH = 192
DIM = 384
HEADS = 16
SPLIT = 8
ROWS = 256
COLS = 256


def draw_qkv_weight(key, part):
    first, second = jax.random.split(key, 2)
    base = jax.random.truncated_normal(first, -3.0, 3.0, (DIM, 3 * DIM), jnp.float32)
    head_scale = jnp.exp(jax.random.uniform(second, (HEADS,), jnp.float32, math.log(1.2), math.log(2.2)))
    per_column = jnp.repeat(head_scale, DIM // HEADS)
    column_scale = jnp.concatenate([per_column, per_column, jnp.ones((DIM,), jnp.float32)])
    return (base * column_scale[None, :] / math.sqrt(DIM)).astype(jnp.bfloat16)


def shard_levels(stream_key, shape, pieces, least, top_value):
    level = 1.0
    for dim, shards_of in pieces:
        steps = jax.random.uniform(jax.random.fold_in(jax.random.fold_in(stream_key, 6), dim), (shards_of,), jnp.float32, least / len(pieces), top_value / len(pieces))
        level = level * jnp.repeat(jnp.exp(steps), shape[dim] // shards_of).reshape((-1,) + (1,) * (len(shape) - 1 - dim))
    return level


def normal_values(own_key, shape, scale, most, shards=(), held_as=jnp.bfloat16):
    entries = scale * jax.random.normal(own_key, shape, jnp.float32)
    if shards:
        entries = entries * shard_levels(own_key, shape, shards, -0.22, 0.18)
    return jnp.clip(entries, -most, most).astype(held_as)


def setup_inputs(seed: int = 0) -> dict:
    keys = jax.random.split(jax.random.key(seed), 11)
    image = normal_values(keys[0], (2 * ROWS, 2 * COLS, IN_CH), 1.0, 6.0, ((0, 16), (1, 16)))
    conv_weight = normal_values(keys[1], (3, 3, IN_CH, DIM), (9 * IN_CH) ** -0.5, 0.15625)
    conv_bias = normal_values(keys[2], (DIM,), 0.5, 3.0, (), jnp.float32)
    merge_gain = jnp.clip(1.0 + 0.15 * jax.random.normal(keys[3], (DIM,), jnp.float32), 0.25, 1.75)
    merge_shift = normal_values(keys[4], (DIM,), 0.5, 3.0, (), jnp.float32)
    norm_gain = jnp.clip(1.0 + 0.15 * jax.random.normal(keys[5], (DIM,), jnp.float32), 0.25, 1.75)
    norm_shift = normal_values(keys[6], (DIM,), 0.5, 3.0, (), jnp.float32)
    qkv_weight = draw_qkv_weight(jax.random.fold_in(keys[10], 71), 0)
    proj_weight = normal_values(keys[8], (DIM, DIM), DIM ** -0.5, 0.3125)
    proj_bias = normal_values(keys[9], (DIM,), 0.5, 3.0, (), jnp.float32)
    return {"image": image, "conv_weight": conv_weight, "conv_bias": conv_bias, "merge_gain": merge_gain, "merge_shift": merge_shift, "norm_gain": norm_gain, "norm_shift": norm_shift, "qkv_weight": qkv_weight, "proj_weight": proj_weight, "proj_bias": proj_bias}


def layer_norm(values, gain, shift):
    center = values - lax.optimization_barrier(jnp.mean(values, -1, keepdims=True))
    spread = lax.optimization_barrier(jnp.mean(center * center, -1, keepdims=True))
    return center * lax.rsqrt(spread + 1e-05) * gain + shift

def stripe_attention(block):
    wide = block.astype(jnp.float32)
    queries = wide[:, 0].transpose(1, 0, 2)
    key_rows = wide[:, 1].transpose(1, 0, 2)
    value_rows = wide[:, 2].transpose(1, 0, 2)
    scores = jnp.einsum('hqd,hkd->hqk', queries, key_rows) / math.sqrt(queries.shape[-1])
    highest = lax.optimization_barrier(jnp.max(scores, -1, keepdims=True))
    weights = jnp.exp(scores - highest)
    totals = lax.optimization_barrier(jnp.sum(weights, -1, keepdims=True))
    probs = lax.optimization_barrier(weights.astype(jnp.bfloat16)).astype(jnp.float32)
    mixed = jnp.einsum('hqk,hkd->hqd', probs, value_rows)
    return (mixed / totals).astype(jnp.bfloat16).transpose(1, 0, 2)

def reference(image, conv_weight, conv_bias, merge_gain, merge_shift, norm_gain, norm_shift, qkv_weight, proj_weight, proj_bias):
    heads_half = HEADS // 2
    depth = DIM // HEADS
    merged = lax.conv_general_dilated(image.astype(jnp.float32)[None], conv_weight.astype(jnp.float32), (2, 2), ((1, 0), (1, 0)), dimension_numbers=('NHWC', 'HWIO', 'NHWC'), precision=lax.Precision.HIGHEST)[0]
    merged = merged + conv_bias
    tokens = layer_norm(merged, merge_gain, merge_shift).astype(jnp.bfloat16)
    normed = layer_norm(tokens.astype(jnp.float32), norm_gain, norm_shift).astype(jnp.bfloat16)
    qkv = jnp.dot(normed.reshape(ROWS * COLS, DIM), qkv_weight, preferred_element_type=jnp.float32)
    qkv = qkv.astype(jnp.bfloat16).reshape(ROWS, COLS, 3, 2, heads_half, depth)
    row_blocks = qkv[:, :, :, 0].reshape(ROWS // SPLIT, SPLIT * COLS, 3, heads_half, depth)
    row_out = lax.map(stripe_attention, row_blocks).reshape(ROWS, COLS, heads_half, depth)
    col_blocks = qkv[:, :, :, 1].reshape(ROWS, COLS // SPLIT, SPLIT, 3, heads_half, depth)
    col_blocks = col_blocks.transpose(1, 0, 2, 3, 4, 5).reshape(COLS // SPLIT, ROWS * SPLIT, 3, heads_half, depth)
    col_out = lax.map(stripe_attention, col_blocks).reshape(COLS // SPLIT, ROWS, SPLIT, heads_half, depth)
    col_out = col_out.transpose(1, 0, 2, 3, 4).reshape(ROWS, COLS, heads_half, depth)
    attention = jnp.concatenate([row_out, col_out], 2).reshape(ROWS * COLS, DIM)
    output = tokens.astype(jnp.float32).reshape(ROWS * COLS, DIM)
    output = output + jnp.dot(attention, proj_weight, preferred_element_type=jnp.float32) + proj_bias
    return output.astype(jnp.bfloat16).reshape(ROWS, COLS, DIM)
```

```python
import functools
import math

import jax
import jax.numpy as jnp
from jax import lax
from jax.experimental import pallas as pl
from jax.experimental.pallas import tpu as pltpu
from jax.sharding import PartitionSpec as P

HEADS = 16
SPLIT = 8
PEERS = 16
DEPTH = 24
BLOCK = 80
BACK = 32
HALF = 192
DIM = 384
TOKENS = 256
F32 = jnp.float32
BF16 = jnp.bfloat16
MESH = pl.DeviceIdType.MESH


def layer_norm(values, gain, shift):
    center = values - jnp.mean(values, -1, keepdims=True)
    spread = jnp.mean(center * center, -1, keepdims=True)
    return center * lax.rsqrt(spread + 1e-05) * gain + shift


def by_stripe(values):
    pieces = [values[16 * i + 8 * s : 16 * i + 8 * s + 8] for s in range(2) for i in range(16)]
    return jnp.concatenate(pieces, 0)


def by_row(values):
    pieces = [values[128 * s + 8 * i : 128 * s + 8 * i + 8] for i in range(16) for s in range(2)]
    return jnp.concatenate(pieces, 0)


def kernel(
    image_hbm, conv_hbm, qkv_hbm, proj_hbm,
    conv_bias, merge_gain, merge_shift, norm_gain, norm_shift, proj_bias,
    out_ref,
    image, conv_w, qkv_w, proj_w, padded, phases, qkv_t,
    column, halo_row, halo_col, halo_corner,
    send_r, recv_r, send_c, recv_c,
    back_send_r, back_recv_r, back_send_c, back_recv_c,
    query_t, keys, value_t, scores, tokens_ref,
    load_sem, halo_send, halo_recv,
    send_sem, recv_sem, back_send_sem, back_recv_sem,
):
    me_r = lax.axis_index("row")
    me_c = lax.axis_index("col")
    down, up = lax.rem(me_r + 1, PEERS), lax.rem(me_r + PEERS - 1, PEERS)
    right, left = lax.rem(me_c + 1, PEERS), lax.rem(me_c + PEERS - 1, PEERS)

    loads = [
        pltpu.make_async_copy(image_hbm, image, load_sem.at[0]),
        pltpu.make_async_copy(qkv_hbm, qkv_w, load_sem.at[1]),
        pltpu.make_async_copy(conv_hbm, conv_w, load_sem.at[2]),
        pltpu.make_async_copy(proj_hbm, proj_w, load_sem.at[3]),
    ]
    for load in loads:
        load.start()

    barrier = pltpu.get_barrier_semaphore()
    for step in range(1, PEERS):
        pl.semaphore_signal(barrier, inc=1, device_id=(me_r, lax.rem(me_c + step, PEERS)), device_id_type=MESH)
        pl.semaphore_signal(barrier, inc=1, device_id=(lax.rem(me_r + step, PEERS), me_c), device_id_type=MESH)
    pl.semaphore_signal(barrier, inc=1, device_id=(down, right), device_id_type=MESH)
    pl.semaphore_signal(barrier, inc=1, device_id=(up, left), device_id_type=MESH)

    loads[0].wait()
    def pad(rows, cols, values):
        padded[0, rows, cols, :] = values[:, :, 0:128]
        padded[1, rows, cols, 0:64] = values[:, :, 128:192]

    pad(slice(1, 33), slice(8, 40), image[...].astype(F32))
    column[:, 0:128] = padded[0, 1:33, 39:40, :].reshape(32, 128).astype(BF16)
    column[:, 128:192] = padded[1, 1:33, 39:40, 0:64].reshape(32, 64).astype(BF16)
    loads[1].wait()
    qkv_t[...] = qkv_w[...].T

    pl.semaphore_wait(barrier, 2 * (PEERS - 1) + 2)
    halos = [
        pltpu.make_async_remote_copy(
            src_ref=image.at[31], dst_ref=halo_row, send_sem=halo_send.at[0], recv_sem=halo_recv.at[0],
            device_id=(down, me_c), device_id_type=MESH),
        pltpu.make_async_remote_copy(
            src_ref=column, dst_ref=halo_col, send_sem=halo_send.at[1], recv_sem=halo_recv.at[1],
            device_id=(me_r, right), device_id_type=MESH),
        pltpu.make_async_remote_copy(
            src_ref=column.at[pl.ds(16, 16)], dst_ref=halo_corner, send_sem=halo_send.at[2], recv_sem=halo_recv.at[2],
            device_id=(down, right), device_id_type=MESH),
    ]
    for halo in halos:
        halo.start()
    loads[2].wait()
    loads[3].wait()
    for halo in halos:
        halo.wait()

    has_up, has_left = me_r > 0, me_c > 0
    pad(slice(0, 1), slice(8, 40), jnp.where(has_up, halo_row[...].astype(F32), 0.0)[None])
    pad(slice(1, 33), slice(7, 8), jnp.where(has_left, halo_col[...].astype(F32), 0.0).reshape(32, 1, 192))
    corner = halo_corner[...].astype(F32)[15:16]
    pad(slice(0, 1), slice(7, 8), jnp.where(jnp.logical_and(has_up, has_left), corner, 0.0)[None])
    for tap in range(3):
        low = padded[0, :, pl.ds(7 + tap, 16, stride=2), :].astype(BF16)
        high = padded[1, :, pl.ds(7 + tap, 16, stride=2), :].astype(BF16)
        phases[tap, :, :, :, 0:128] = low.reshape(17, 2, 16, 128)
        phases[tap, :, :, :, 128:192] = high[:, :, 0:64].reshape(17, 2, 16, 64)
    merged = jnp.zeros((TOKENS, DIM), F32)
    for a in range(3):
        for b in range(3):
            window = phases[b, pl.ds(a // 2, 16), a % 2].reshape(TOKENS, 192)
            merged = merged + jnp.dot(window, conv_w[a, b], preferred_element_type=F32)
    merged = merged + conv_bias[...][None, :]
    tokens = layer_norm(merged, merge_gain[...][None, :], merge_shift[...][None, :]).astype(BF16)
    tokens_ref[...] = tokens
    normed = layer_norm(tokens.astype(F32), norm_gain[...][None, :], norm_shift[...][None, :])

    ones = jnp.ones((8, TOKENS), F32)

    def project(normed_half, base, send):
        parts = [
            lax.dot_general(
                qkv_t[part * DIM + base : part * DIM + base + HALF, :], normed_half,
                (((1,), (1,)), ((), ())), preferred_element_type=F32)
            for part in range(3)
        ]
        for head in range(HEADS // 2):
            rows = slice(DEPTH * head, DEPTH * head + DEPTH)
            block = jnp.concatenate([part[rows] for part in parts] + [ones], 0).astype(BF16)
            send[head] = block[:, :128]
            send[8 + head] = block[:, 128:]

    def leave(axis, me, send, recv, phase, sends, recvs, peer):
        return pltpu.make_async_remote_copy(
            src_ref=send.at[peer], dst_ref=recv.at[me],
            send_sem=sends.at[phase, peer], recv_sem=recvs.at[phase, me],
            device_id=(me_r, peer) if axis == "col" else (peer, me_c), device_id_type=MESH)

    def arrive(axis, me, send, recv, phase, sends, recvs, peer):
        return pltpu.make_async_remote_copy(
            src_ref=send.at[peer], dst_ref=recv.at[peer],
            send_sem=sends.at[phase, peer], recv_sem=recvs.at[phase, peer],
            device_id=(me_r, peer) if axis == "col" else (peer, me_c), device_id_type=MESH)

    def start_all(axis, me, send, recv, phase):
        for step in range(1, PEERS):
            peer = lax.rem(me + step, PEERS)
            leave(axis, me, send, recv, phase, send_sem, recv_sem, peer).start()

    def wait_all(axis, me, send, recv, phase, sends, recvs, sent):
        for step in range(1, PEERS):
            peer = lax.rem(me + step, PEERS)
            if sent:
                leave(axis, me, send, recv, phase, sends, recvs, peer).wait_send()
            else:
                arrive(axis, me, send, recv, phase, sends, recvs, peer).wait_recv()

    project(normed.astype(BF16), 0, send_r)
    start_all("col", me_c, send_r, recv_r, 0)
    project(by_stripe(normed).astype(BF16), HALF, send_c)
    start_all("row", me_r, send_c, recv_c, 1)

    def attend(axis, me, send, recv, back_send, back_recv, phase):
        recv[me] = send[me]
        wait_all(axis, me, send, recv, phase, send_sem, recv_sem, False)
        for peer in range(PEERS):
            lanes = slice(128 * peer, 128 * peer + 128)
            query_t[:, lanes] = recv[peer, 0:32, :]
            value_t[:, lanes] = recv[peer, 48:80, :]
            own = recv[peer, 0:48, :].astype(F32)[24:48]
            own = jnp.concatenate([own, jnp.zeros((104, 128), F32)], 0)
            keys[lanes, :] = own.T.astype(BF16)
        mine = me // 2

        def tile(step, carry):
            place = lax.rem(mine + 1 + step, 8)
            start = pl.multiple_of(place * 256, 256)
            query = query_t[:, pl.ds(start, 256)]
            highest = jnp.full((8, 256), -jnp.inf, F32)
            for chunk in range(8):
                rows = slice(256 * chunk, 256 * chunk + 256)
                part = jnp.dot(keys[rows, 0:32], query, preferred_element_type=F32)
                scores[rows, :] = part
                highest = jnp.maximum(highest, jnp.max(part.reshape(32, 8, 256), 0))
            highest = jnp.max(highest, 0, keepdims=True)
            summed = jnp.zeros((32, 256), F32)
            for chunk in range(8):
                rows = slice(256 * chunk, 256 * chunk + 256)
                weights = jnp.exp((scores[rows, :] - highest) * (1.0 / math.sqrt(DEPTH)))
                summed = summed + jnp.dot(value_t[:, rows], weights.astype(BF16), preferred_element_type=F32)
            result = summed[0:24] / summed[24:25]
            result = jnp.concatenate([result, jnp.zeros((8, 256), F32)], 0).astype(BF16)
            back_send[2 * place] = result[:, :128]
            back_send[2 * place + 1] = result[:, 128:]
            for half in range(2):
                peer = 2 * place + half

                @pl.when(peer != me)
                def _():
                    leave(axis, me, back_send, back_recv, phase, back_send_sem, back_recv_sem, peer).start()

            return carry

        lax.fori_loop(0, 8, tile, 0)
        back_recv[me] = back_send[me]

    def mix(back_recv, base):
        outs = []
        for stripe in range(2):
            heads = [back_recv[8 * stripe + head].astype(F32)[0:24] for head in range(8)]
            mixed = jnp.concatenate(heads, 0).T.astype(BF16)
            outs.append(jnp.dot(mixed, proj_w[base : base + HALF, :], preferred_element_type=F32))
        return jnp.concatenate(outs, 0)

    attend("col", me_c, send_r, recv_r, back_send_r, back_recv_r, 0)
    attend("row", me_r, send_c, recv_c, back_send_c, back_recv_c, 1)
    wait_all("col", me_c, back_send_r, back_recv_r, 0, back_send_sem, back_recv_sem, False)
    total = mix(back_recv_r, 0) + tokens_ref[...].astype(F32) + proj_bias[...][None, :]
    wait_all("row", me_r, back_send_c, back_recv_c, 1, back_send_sem, back_recv_sem, False)
    total = (total + by_row(mix(back_recv_c, HALF))).astype(BF16)
    out_ref[...] = total.reshape(16, 16, DIM)
    wait_all("col", me_c, send_r, recv_r, 0, send_sem, recv_sem, True)
    wait_all("row", me_r, send_c, recv_c, 1, send_sem, recv_sem, True)
    wait_all("col", me_c, back_send_r, back_recv_r, 0, back_send_sem, back_recv_sem, True)
    wait_all("row", me_r, back_send_c, back_recv_c, 1, back_send_sem, back_recv_sem, True)


def on_device(image, conv_weight, conv_bias, merge_gain, merge_shift, norm_gain, norm_shift, qkv_weight, proj_weight, proj_bias):
    anyspace = pl.BlockSpec(memory_space=pl.ANY)
    vmem = pl.BlockSpec(memory_space=pltpu.VMEM)
    return pl.pallas_call(
        kernel,
        out_shape=jax.ShapeDtypeStruct((16, 16, DIM), BF16),
        in_specs=[anyspace] * 4 + [vmem] * 6,
        out_specs=vmem,
        scratch_shapes=[
            pltpu.VMEM((32, 32, 192), BF16),
            pltpu.VMEM((3, 3, 192, DIM), BF16),
            pltpu.VMEM((DIM, 3 * DIM), BF16),
            pltpu.VMEM((DIM, DIM), BF16),
            pltpu.VMEM((2, 34, 40, 128), F32),
            pltpu.VMEM((3, 17, 2, 16, 192), BF16),
            pltpu.VMEM((3 * DIM, DIM), BF16),
            pltpu.VMEM((32, 192), BF16),
            pltpu.VMEM((32, 192), BF16),
            pltpu.VMEM((32, 192), BF16),
            pltpu.VMEM((16, 192), BF16),
        ]
        + [pltpu.VMEM((PEERS, BLOCK, 128), BF16)] * 4
        + [pltpu.VMEM((PEERS, BACK, 128), BF16)] * 4
        + [
            pltpu.VMEM((32, 2048), BF16),
            pltpu.VMEM((2048, 128), BF16),
            pltpu.VMEM((32, 2048), BF16),
            pltpu.VMEM((2048, 256), F32),
            pltpu.VMEM((TOKENS, DIM), BF16),
            pltpu.SemaphoreType.DMA((4,)),
            pltpu.SemaphoreType.DMA((3,)),
            pltpu.SemaphoreType.DMA((3,)),
            pltpu.SemaphoreType.DMA((2, PEERS)),
            pltpu.SemaphoreType.DMA((2, PEERS)),
            pltpu.SemaphoreType.DMA((2, PEERS)),
            pltpu.SemaphoreType.DMA((2, PEERS)),
        ],
        compiler_params=pltpu.CompilerParams(
            collective_id=0, has_side_effects=True, vmem_limit_bytes=48 << 20),
    )(image, conv_weight, qkv_weight, proj_weight, conv_bias, merge_gain, merge_shift, norm_gain, norm_shift, proj_bias)


def solution(mesh):
    return jax.shard_map(
        on_device,
        mesh=mesh,
        in_specs=(P("row", "col", None), P(), P(), P(), P(), P(), P(), P(), P(), P()),
        out_specs=P("row", "col", None),
        check_vma=False,
    )
```

```python
import functools
import math

import jax
import jax.numpy as jnp
from jax import lax
from jax.experimental import pallas as pl
from jax.experimental.pallas import tpu as pltpu
from jax.sharding import PartitionSpec as P

HEADS = 16
SPLIT = 8
PEERS = 16
DEPTH = 24
BLOCK = 72
BACK = 24
HALF = 192
DIM = 384
CHUNK = 512
TOKENS = 256
F32 = jnp.float32
BF16 = jnp.bfloat16
MESH = pl.DeviceIdType.MESH


def layer_norm(values, gain, shift):
    center = values - jnp.mean(values, -1, keepdims=True)
    spread = jnp.mean(center * center, -1, keepdims=True)
    return center * lax.rsqrt(spread + 1e-05) * gain + shift


def by_stripe(values):
    pieces = [values[16 * i + 8 * s : 16 * i + 8 * s + 8] for s in range(2) for i in range(16)]
    return jnp.concatenate(pieces, 0)


def by_row(values):
    pieces = [values[128 * s + 8 * i : 128 * s + 8 * i + 8] for i in range(16) for s in range(2)]
    return jnp.concatenate(pieces, 0)


def kernel(
    image_hbm, conv_hbm, qkv_hbm, proj_hbm,
    conv_bias_hbm, merge_gain_hbm, merge_shift_hbm, norm_gain_hbm, norm_shift_hbm, proj_bias_hbm,
    out_ref,
    conv_bias, merge_gain, merge_shift, norm_gain, norm_shift, proj_bias,
    image, conv_w, qkv_w, proj_w, padded, phases, qkv_t,
    column, halo_row, halo_col, halo_corner,
    send_r, recv_r, send_c, recv_c,
    back_send_r, back_recv_r, back_send_c, back_recv_c,
    query_t, keys, value_t, scores, tokens_ref,
    load_sem, halo_send, halo_recv,
    send_sem, recv_sem, back_send_sem, back_recv_sem,
):
    me_r = lax.axis_index("row")
    me_c = lax.axis_index("col")
    down, up = lax.rem(me_r + 1, PEERS), lax.rem(me_r + PEERS - 1, PEERS)
    right, left = lax.rem(me_c + 1, PEERS), lax.rem(me_c + PEERS - 1, PEERS)

    barrier = pltpu.get_barrier_semaphore()
    for step in range(1, PEERS):
        pl.semaphore_signal(barrier, inc=1, device_id=(me_r, lax.rem(me_c + step, PEERS)), device_id_type=MESH)
        pl.semaphore_signal(barrier, inc=1, device_id=(lax.rem(me_r + step, PEERS), me_c), device_id_type=MESH)
    pl.semaphore_signal(barrier, inc=1, device_id=(down, right), device_id_type=MESH)
    pl.semaphore_signal(barrier, inc=1, device_id=(up, left), device_id_type=MESH)

    loads = [
        pltpu.make_async_copy(image_hbm, image, load_sem.at[0]),
        pltpu.make_async_copy(qkv_hbm, qkv_w, load_sem.at[1]),
        pltpu.make_async_copy(conv_hbm, conv_w, load_sem.at[2]),
        pltpu.make_async_copy(proj_hbm, proj_w, load_sem.at[3]),
    ]
    vectors = [
        pltpu.make_async_copy(source, target, load_sem.at[4 + place])
        for place, (source, target) in enumerate([
            (conv_bias_hbm, conv_bias), (merge_gain_hbm, merge_gain), (merge_shift_hbm, merge_shift),
            (norm_gain_hbm, norm_gain), (norm_shift_hbm, norm_shift), (proj_bias_hbm, proj_bias)])
    ]
    for load in loads + vectors:
        load.start()

    loads[0].wait()
    def pad(rows, cols, values):
        padded[0, rows, cols, :] = values[:, :, 0:128]
        padded[1, rows, cols, 0:64] = values[:, :, 128:192]

    pad(slice(1, 33), slice(8, 40), image[...].astype(F32))
    column[:, 0:128] = padded[0, 1:33, 39:40, :].reshape(32, 128).astype(BF16)
    column[:, 128:192] = padded[1, 1:33, 39:40, 0:64].reshape(32, 64).astype(BF16)
    loads[1].wait()
    qkv_t[...] = qkv_w[...].T
    value_t[24:32, :] = jnp.ones((8, 2048), BF16)

    pl.semaphore_wait(barrier, 2 * (PEERS - 1) + 2)
    halos = [
        pltpu.make_async_remote_copy(
            src_ref=image.at[31], dst_ref=halo_row, send_sem=halo_send.at[0], recv_sem=halo_recv.at[0],
            device_id=(down, me_c), device_id_type=MESH),
        pltpu.make_async_remote_copy(
            src_ref=column, dst_ref=halo_col, send_sem=halo_send.at[1], recv_sem=halo_recv.at[1],
            device_id=(me_r, right), device_id_type=MESH),
        pltpu.make_async_remote_copy(
            src_ref=column.at[pl.ds(16, 16)], dst_ref=halo_corner, send_sem=halo_send.at[2], recv_sem=halo_recv.at[2],
            device_id=(down, right), device_id_type=MESH),
    ]
    for halo in halos:
        halo.start()
    for load in loads[2:] + vectors:
        load.wait()
    for halo in halos:
        halo.wait()

    has_up, has_left = me_r > 0, me_c > 0
    pad(slice(0, 1), slice(8, 40), jnp.where(has_up, halo_row[...].astype(F32), 0.0)[None])
    pad(slice(1, 33), slice(7, 8), jnp.where(has_left, halo_col[...].astype(F32), 0.0).reshape(32, 1, 192))
    corner = halo_corner[...].astype(F32)[15:16]
    pad(slice(0, 1), slice(7, 8), jnp.where(jnp.logical_and(has_up, has_left), corner, 0.0)[None])
    for tap in range(3):
        low = padded[0, :, pl.ds(7 + tap, 16, stride=2), :].astype(BF16)
        high = padded[1, :, pl.ds(7 + tap, 16, stride=2), :].astype(BF16)
        phases[tap, :, :, :, 0:128] = low.reshape(17, 2, 16, 128)
        phases[tap, :, :, :, 128:192] = high[:, :, 0:64].reshape(17, 2, 16, 64)
    merged = jnp.zeros((TOKENS, DIM), F32)
    for a in range(3):
        for b in range(3):
            window = phases[b, pl.ds(a // 2, 16), a % 2].reshape(TOKENS, 192)
            merged = merged + jnp.dot(window, conv_w[a, b], preferred_element_type=F32)
    merged = merged + conv_bias[...][None, :]
    tokens = layer_norm(merged, merge_gain[...][None, :], merge_shift[...][None, :]).astype(BF16)
    tokens_ref[...] = tokens
    normed = layer_norm(tokens.astype(F32), norm_gain[...][None, :], norm_shift[...][None, :])

    def project(normed_half, base, send):
        parts = [
            lax.dot_general(
                qkv_t[part * DIM + base : part * DIM + base + HALF, :], normed_half,
                (((1,), (1,)), ((), ())), preferred_element_type=F32)
            for part in range(3)
        ]
        for head in range(HEADS // 2):
            rows = slice(DEPTH * head, DEPTH * head + DEPTH)
            block = jnp.concatenate([part[rows] for part in parts], 0).astype(BF16)
            send[head] = block[:, :128]
            send[8 + head] = block[:, 128:]

    def leave(axis, me, send, recv, phase, sends, recvs, peer):
        return pltpu.make_async_remote_copy(
            src_ref=send.at[peer], dst_ref=recv.at[me],
            send_sem=sends.at[phase, peer], recv_sem=recvs.at[phase, me],
            device_id=(me_r, peer) if axis == "col" else (peer, me_c), device_id_type=MESH)

    def arrive(axis, me, send, recv, phase, sends, recvs, peer):
        return pltpu.make_async_remote_copy(
            src_ref=send.at[peer], dst_ref=recv.at[peer],
            send_sem=sends.at[phase, peer], recv_sem=recvs.at[phase, peer],
            device_id=(me_r, peer) if axis == "col" else (peer, me_c), device_id_type=MESH)

    def start_all(axis, me, send, recv, phase):
        for step in range(1, PEERS):
            peer = lax.rem(me + step, PEERS)
            leave(axis, me, send, recv, phase, send_sem, recv_sem, peer).start()

    def wait_all(axis, me, send, recv, phase, sends, recvs, sent):
        for step in range(1, PEERS):
            peer = lax.rem(me + step, PEERS)
            if sent:
                leave(axis, me, send, recv, phase, sends, recvs, peer).wait_send()
            else:
                arrive(axis, me, send, recv, phase, sends, recvs, peer).wait_recv()

    project(normed.astype(BF16), 0, send_r)
    start_all("col", me_c, send_r, recv_r, 0)
    project(by_stripe(normed).astype(BF16), HALF, send_c)
    start_all("row", me_r, send_c, recv_c, 1)

    def attend(axis, me, send, recv, back_send, back_recv, phase):
        recv[me] = send[me]
        wait_all(axis, me, send, recv, phase, send_sem, recv_sem, False)
        for peer in range(PEERS):
            lanes = slice(128 * peer, 128 * peer + 128)
            query_t[:, lanes] = recv[peer, 0:32, :]
            value_t[0:24, lanes] = recv[peer, 48:72, :]
            own = recv[peer, 0:48, :].astype(F32)[24:48]
            own = jnp.concatenate([own, jnp.zeros((104, 128), F32)], 0)
            keys[lanes, :] = own.T.astype(BF16)
        outer, inner = (me // 4, lax.rem(me // 2, 2)) if axis == "col" else (me // 4, lax.rem(me, 4) // 2)
        places = []
        for inner_step in (1, 0):
            for outer_step in (2, 1, 3, 0):
                places.append(lax.rem(outer + outer_step, 4) * 2 + lax.rem(inner + inner_step, 2))

        def score(query, buffer, chunk, highest):
            rows = slice(CHUNK * chunk, CHUNK * chunk + CHUNK)
            part = jnp.dot(keys[rows, 0:32], query, preferred_element_type=F32)
            scores[buffer, rows, :] = part
            return jnp.maximum(highest, jnp.max(part.reshape(CHUNK // 8, 8, 256), 0))

        def gather(buffer, chunk, highest, summed):
            rows = slice(CHUNK * chunk, CHUNK * chunk + CHUNK)
            weights = jnp.exp2((scores[buffer, rows, :] - highest) * (math.log2(math.e) / math.sqrt(DEPTH)))
            return summed + jnp.dot(value_t[:, rows], weights.astype(BF16), preferred_element_type=F32)

        def finish(place, summed):
            result = (summed[0:24] / summed[24:25]).astype(BF16)
            back_send[2 * place] = result[:, :128]
            back_send[2 * place + 1] = result[:, 128:]
            for half in range(2):
                peer = 2 * place + half

                @pl.when(peer != me)
                def _():
                    leave(axis, me, back_send, back_recv, phase, back_send_sem, back_recv_sem, peer).start()

        highest = None
        for step in range(9):
            later = jnp.full((8, 256), -jnp.inf, F32)
            summed = jnp.zeros((32, 256), F32)
            if step < 8:
                query = query_t[:, pl.ds(pl.multiple_of(places[step] * 256, 256), 256)]
            for chunk in range(2048 // CHUNK):
                if step < 8:
                    later = score(query, step % 2, chunk, later)
                if step > 0:
                    summed = gather((step - 1) % 2, chunk, highest, summed)
            if step > 0:
                finish(places[step - 1], summed)
            highest = jnp.max(later, 0, keepdims=True)
        back_recv[me] = back_send[me]

    def mix(back_recv, base):
        outs = []
        for stripe in range(2):
            heads = [back_recv[8 * stripe + head].astype(F32) for head in range(8)]
            mixed = jnp.concatenate(heads, 0).T.astype(BF16)
            outs.append(jnp.dot(mixed, proj_w[base : base + HALF, :], preferred_element_type=F32))
        return jnp.concatenate(outs, 0)

    attend("col", me_c, send_r, recv_r, back_send_r, back_recv_r, 0)
    attend("row", me_r, send_c, recv_c, back_send_c, back_recv_c, 1)
    wait_all("col", me_c, back_send_r, back_recv_r, 0, back_send_sem, back_recv_sem, False)
    total = mix(back_recv_r, 0) + tokens_ref[...].astype(F32) + proj_bias[...][None, :]
    wait_all("row", me_r, back_send_c, back_recv_c, 1, back_send_sem, back_recv_sem, False)
    total = (total + by_row(mix(back_recv_c, HALF))).astype(BF16)
    out_ref[...] = total.reshape(16, 16, DIM)
    wait_all("col", me_c, send_r, recv_r, 0, send_sem, recv_sem, True)
    wait_all("row", me_r, send_c, recv_c, 1, send_sem, recv_sem, True)
    wait_all("col", me_c, back_send_r, back_recv_r, 0, back_send_sem, back_recv_sem, True)
    wait_all("row", me_r, back_send_c, back_recv_c, 1, back_send_sem, back_recv_sem, True)


def on_device(image, conv_weight, conv_bias, merge_gain, merge_shift, norm_gain, norm_shift, qkv_weight, proj_weight, proj_bias):
    anyspace = pl.BlockSpec(memory_space=pltpu.HBM)
    vmem = pl.BlockSpec(memory_space=pltpu.VMEM)
    return pl.pallas_call(
        kernel,
        out_shape=jax.ShapeDtypeStruct((16, 16, DIM), BF16),
        in_specs=[anyspace] * 10,
        out_specs=vmem,
        scratch_shapes=[pltpu.VMEM((DIM,), F32)] * 6
        + [
            pltpu.VMEM((32, 32, 192), BF16),
            pltpu.VMEM((3, 3, 192, DIM), BF16),
            pltpu.VMEM((DIM, 3 * DIM), BF16),
            pltpu.VMEM((DIM, DIM), BF16),
            pltpu.VMEM((2, 34, 40, 128), F32),
            pltpu.VMEM((3, 17, 2, 16, 192), BF16),
            pltpu.VMEM((3 * DIM, DIM), BF16),
            pltpu.VMEM((32, 192), BF16),
            pltpu.VMEM((32, 192), BF16),
            pltpu.VMEM((32, 192), BF16),
            pltpu.VMEM((16, 192), BF16),
        ]
        + [pltpu.VMEM((PEERS, BLOCK, 128), BF16)] * 4
        + [pltpu.VMEM((PEERS, BACK, 128), BF16)] * 4
        + [
            pltpu.VMEM((32, 2048), BF16),
            pltpu.VMEM((2048, 128), BF16),
            pltpu.VMEM((32, 2048), BF16),
            pltpu.VMEM((2, 2048, 256), F32),
            pltpu.VMEM((TOKENS, DIM), BF16),
            pltpu.SemaphoreType.DMA((10,)),
            pltpu.SemaphoreType.DMA((3,)),
            pltpu.SemaphoreType.DMA((3,)),
            pltpu.SemaphoreType.DMA((2, PEERS)),
            pltpu.SemaphoreType.DMA((2, PEERS)),
            pltpu.SemaphoreType.DMA((2, PEERS)),
            pltpu.SemaphoreType.DMA((2, PEERS)),
        ],
        compiler_params=pltpu.CompilerParams(
            collective_id=0, has_side_effects=True, vmem_limit_bytes=67043328),
    )(image, conv_weight, qkv_weight, proj_weight, conv_bias, merge_gain, merge_shift, norm_gain, norm_shift, proj_bias)


def solution(mesh):
    return jax.shard_map(
        on_device,
        mesh=mesh,
        in_specs=(P("row", "col", None), P(), P(), P(), P(), P(), P(), P(), P(), P()),
        out_specs=P("row", "col", None),
        check_vma=False,
    )
```

```python
import math

import jax
import jax.numpy as jnp
from jax import lax
from jax.experimental import pallas as pl
from jax.experimental.pallas import tpu as pltpu
from jax.sharding import PartitionSpec as P

HEADS = 16
PEERS = 16
DEPTH = 24
HALF = 192
DIM = 384
TOKENS = 256
CHUNK = 512
F32 = jnp.float32
BF16 = jnp.bfloat16
MESH = pl.DeviceIdType.MESH
FAR_FIRST = (2, 1, 3, 0)


def layer_norm(values, gain, shift):
    center = values - jnp.mean(values, -1, keepdims=True)
    spread = jnp.mean(center * center, -1, keepdims=True)
    return center * lax.rsqrt(spread + 1e-05) * gain + shift


def by_stripe(values):
    pieces = [values[16 * i + 8 * s : 16 * i + 8 * s + 8] for s in range(2) for i in range(16)]
    return jnp.concatenate(pieces, 0)


def by_row(values):
    pieces = [values[128 * s + 8 * i : 128 * s + 8 * i + 8] for i in range(16) for s in range(2)]
    return jnp.concatenate(pieces, 0)


def lanes_in(refs, rows):
    return jnp.concatenate([ref[rows, :] for ref in refs], 1)


def kernel(
    image_hbm, conv_hbm, qkv_hbm, proj_hbm,
    conv_bias_hbm, merge_gain_hbm, merge_shift_hbm, norm_gain_hbm, norm_shift_hbm, proj_bias_hbm,
    out_ref,
    conv_bias, merge_gain, merge_shift, norm_gain, norm_shift, proj_bias,
    image, conv_w, qkv_w, proj_w, padded, phases, qkv_t,
    edge_low, edge_high,
    column, halo_row, halo_col, halo_corner,
    merged_0, merged_1, merged_2, tokens_0, tokens_1, tokens_2, normed_0, normed_1, normed_2,
    send_kv, recv_kv, send_q, recv_q, back_send, back_recv,
    keys, value_t, scores,
    load_sem, halo_send, halo_recv,
    kv_send_sem, kv_recv_sem, q_send_sem, q_recv_sem, back_send_sem, back_recv_sem,
):
    me_r = lax.axis_index("row")
    me_c = lax.axis_index("col")
    me = (me_c, me_r)
    down, up = lax.rem(me_r + 1, PEERS), lax.rem(me_r + PEERS - 1, PEERS)
    right, left = lax.rem(me_c + 1, PEERS), lax.rem(me_c + PEERS - 1, PEERS)
    merged_refs = (merged_0, merged_1, merged_2)
    token_refs = (tokens_0, tokens_1, tokens_2)
    normed_refs = (normed_0, normed_1, normed_2)

    def device(axis, peer):
        return (me_r, peer) if axis == 0 else (peer, me_c)

    loads = [
        pltpu.make_async_copy(source, target, load_sem.at[place])
        for place, (source, target) in enumerate([
            (image_hbm, image), (qkv_hbm, qkv_w), (conv_hbm, conv_w), (conv_bias_hbm, conv_bias),
            (merge_gain_hbm, merge_gain), (merge_shift_hbm, merge_shift), (norm_gain_hbm, norm_gain),
            (norm_shift_hbm, norm_shift), (proj_bias_hbm, proj_bias), (proj_hbm, proj_w)])
    ]
    for load in loads:
        load.start()

    peers = ([], [])
    for axis in range(2):
        block, place = me[axis] // 4, lax.rem(me[axis], 4)
        for outer in FAR_FIRST:
            for inner in FAR_FIRST:
                if outer or inner:
                    if axis == 0:
                        peers[0].append(lax.rem(block + outer, 4) * 4 + lax.rem(place + inner, 4))
                    else:
                        peers[1].append(lax.rem(block + inner, 4) * 4 + lax.rem(place + outer, 4))

    barrier = pltpu.get_barrier_semaphore()
    for step in range(PEERS - 1):
        for axis in (1, 0):
            pl.semaphore_signal(barrier, inc=1, device_id=device(axis, peers[axis][step]), device_id_type=MESH)
    pl.semaphore_signal(barrier, inc=1, device_id=(down, right), device_id_type=MESH)
    pl.semaphore_signal(barrier, inc=1, device_id=(up, left), device_id_type=MESH)

    def pad(rows, cols, values):
        padded[0, rows, cols, :] = values[:, :, 0:128]
        padded[1, rows, cols, 0:64] = values[:, :, 128:192]

    pad(slice(0, 1), slice(0, 40), jnp.zeros((1, 40, 192), F32))
    pad(slice(1, 33), slice(0, 8), jnp.zeros((32, 8, 192), F32))
    value_t[0, 24:32, :] = jnp.ones((8, 2048), BF16)
    value_t[1, 24:32, :] = jnp.ones((8, 2048), BF16)
    loads[0].wait()
    pad(slice(1, 33), slice(8, 40), image[...].astype(F32))
    column[:, 0:128] = padded[0, 1:33, 39:40, :].reshape(32, 128).astype(BF16)
    column[:, 128:192] = padded[1, 1:33, 39:40, 0:64].reshape(32, 64).astype(BF16)
    loads[1].wait()
    qkv_t[...] = qkv_w[...].T

    pl.semaphore_wait(barrier, 2 * (PEERS - 1) + 2)
    halos = [
        pltpu.make_async_remote_copy(
            src_ref=image.at[31], dst_ref=halo_row, send_sem=halo_send.at[0], recv_sem=halo_recv.at[0],
            device_id=(down, me_c), device_id_type=MESH),
        pltpu.make_async_remote_copy(
            src_ref=column, dst_ref=halo_col, send_sem=halo_send.at[1], recv_sem=halo_recv.at[1],
            device_id=(me_r, right), device_id_type=MESH),
        pltpu.make_async_remote_copy(
            src_ref=column.at[pl.ds(16, 16)], dst_ref=halo_corner, send_sem=halo_send.at[2], recv_sem=halo_recv.at[2],
            device_id=(down, right), device_id_type=MESH),
    ]
    for halo in halos:
        halo.start()

    for load in loads[2:]:
        load.wait()
    for tap in range(3):
        low = padded[0, :, pl.ds(7 + tap, 16, stride=2), :].astype(BF16)
        high = padded[1, :, pl.ds(7 + tap, 16, stride=2), :].astype(BF16)
        phases[tap, :, :, :, 0:128] = low.reshape(17, 2, 16, 128)
        phases[tap, :, :, :, 128:192] = high[:, :, 0:64].reshape(17, 2, 16, 64)
    merged = jnp.zeros((TOKENS, DIM), F32)
    for a in range(3):
        for b in range(3):
            window = phases[b, pl.ds(a // 2, 16), a % 2].reshape(TOKENS, 192)
            merged = merged + jnp.dot(window, conv_w[a, b], preferred_element_type=F32)

    def norms(values):
        merge_affine = merge_gain[...][None, :], merge_shift[...][None, :]
        tokens = layer_norm(values + conv_bias[...][None, :], *merge_affine).astype(BF16).astype(F32)
        return tokens, layer_norm(tokens, norm_gain[...][None, :], norm_shift[...][None, :])

    def keep(refs, rows, values):
        for place, ref in enumerate(refs):
            ref[rows, :] = values[:, 128 * place : 128 * place + 128]

    tokens, normed = norms(merged)
    keep(merged_refs, slice(None), merged)
    keep(token_refs, slice(None), tokens)
    keep(normed_refs, slice(None), normed)

    for halo in halos:
        halo.wait()
    has_up, has_left = me_r > 0, me_c > 0
    corner = jnp.where(jnp.logical_and(has_up, has_left), halo_corner[...].astype(F32)[15:16], 0.0)
    edge_row = jnp.where(has_up, halo_row[...].astype(F32), 0.0)
    edge_col = jnp.where(has_left, halo_col[...].astype(F32), 0.0)

    def edge_store(rows, values):
        edge_low[rows, :] = values[:, 0:128]
        edge_high[rows, 0:64] = values[:, 128:192]

    def edge_load(start):
        rows = pl.ds(start, 16, stride=2)
        return jnp.concatenate([edge_low[rows, :], edge_high[rows, :][:, 0:64]], 1).astype(BF16)

    edge_store(slice(7, 8), corner)
    edge_store(slice(8, 40), edge_row)
    edge_store(slice(47, 48), jnp.zeros((1, 192), F32))
    edge_store(slice(48, 80), edge_col)
    rows_in = [edge_load(7 + b) for b in range(3)]
    cols_in = [edge_load(47 + a) for a in range(3)]
    shared = jnp.dot(jnp.concatenate([rows_in[0], cols_in[0]], 0), conv_w[0, 0], preferred_element_type=F32)
    row_fix, col_fix = shared[0:16], shared[16:32]
    for tap in (1, 2):
        row_fix = row_fix + jnp.dot(rows_in[tap], conv_w[0, tap], preferred_element_type=F32)
        col_fix = col_fix + jnp.dot(cols_in[tap], conv_w[tap, 0], preferred_element_type=F32)
    first = lax.broadcasted_iota(jnp.int32, (16, DIM), 0) == 0
    row_fix = row_fix + jnp.where(first, col_fix[0:1], 0.0)
    upper, side = slice(0, 16), pl.ds(0, 16, stride=16)
    fixed = jnp.concatenate(
        [lanes_in(merged_refs, upper) + row_fix, lanes_in(merged_refs, side) + col_fix], 0)
    tokens, normed = norms(fixed)
    for refs, values in ((token_refs, tokens), (normed_refs, normed)):
        keep(refs, side, values[16:32])
        keep(refs, upper, values[0:16])
    normed = lanes_in(normed_refs, slice(None))

    def project(values, base, part):
        rows = slice(part * DIM + base, part * DIM + base + HALF)
        return lax.dot_general(qkv_t[rows, :], values, (((1,), (1,)), ((), ())), preferred_element_type=F32)

    def leave(axis, send, recv, sends, recvs, peer):
        return pltpu.make_async_remote_copy(
            src_ref=send.at[axis, peer], dst_ref=recv.at[axis, me[axis]],
            send_sem=sends.at[axis], recv_sem=recvs.at[axis],
            device_id=device(axis, peer), device_id_type=MESH)

    def all_of(axis, send, recv, sends, recvs):
        most = pl.ds(0, PEERS - 1)
        return pltpu.make_async_remote_copy(
            src_ref=send.at[axis, most], dst_ref=recv.at[axis, most],
            send_sem=sends.at[axis], recv_sem=recvs.at[axis],
            device_id=device(axis, peers[axis][0]), device_id_type=MESH)

    kv = (send_kv, recv_kv, kv_send_sem, kv_recv_sem)
    queries = (send_q, recv_q, q_send_sem, q_recv_sem)
    back = (back_send, back_recv, back_send_sem, back_recv_sem)

    for axis in range(2):
        values = (normed if axis == 0 else by_stripe(normed)).astype(BF16)
        key_part, value_part = (project(values, axis * HALF, part) for part in (1, 2))
        for head in range(HEADS // 2):
            rows = slice(DEPTH * head, DEPTH * head + DEPTH)
            block = jnp.concatenate([key_part[rows], value_part[rows]], 0).astype(BF16)
            send_kv[axis, head] = block[:, :128]
            send_kv[axis, 8 + head] = block[:, 128:]
        for peer in peers[axis]:
            leave(axis, *kv, peer).start()
        query_part = project(values, axis * HALF, 0)
        for head in range(HEADS // 2):
            block = query_part[DEPTH * head : DEPTH * head + DEPTH].astype(BF16)
            send_q[axis, head] = block[:, :128]
            send_q[axis, 8 + head] = block[:, 128:]
        for peer in peers[axis] if axis == 0 else []:
            leave(axis, *queries, peer).start()
    for axis in range(2):
        recv_kv[axis, me[axis]] = send_kv[axis, me[axis]]
        recv_q[axis, me[axis]] = send_q[axis, me[axis]]

    def take_keys(axis):
        all_of(axis, *kv).wait_recv()
        for peer in range(PEERS):
            rows = slice(128 * peer, 128 * peer + 128)
            block = recv_kv[axis, peer]
            value_t[axis, 0:24, rows] = block[24:48]
            own = jnp.concatenate([block.astype(F32)[0:24], jnp.zeros((104, 128), F32)], 0)
            keys[axis, rows, :] = own.T.astype(BF16)

    def take_queries(axis, place):
        pair = [2 * place, 2 * place + 1]
        return jnp.concatenate([recv_q[axis, peer] for peer in pair], 1)

    def score(axis, query, buffer, chunk, highest):
        rows = slice(CHUNK * chunk, CHUNK * chunk + CHUNK)
        part = jnp.dot(keys[axis, rows, 0:24], query, preferred_element_type=F32)
        scores[buffer, rows, :] = part
        return jnp.maximum(highest, jnp.max(part.reshape(CHUNK // 8, 8, 256), 0))

    def gather(axis, buffer, chunk, highest, summed):
        rows = slice(CHUNK * chunk, CHUNK * chunk + CHUNK)
        weights = jnp.exp2((scores[buffer, rows, :] - highest) * (math.log2(math.e) / math.sqrt(DEPTH)))
        return summed + jnp.dot(value_t[axis, :, rows], weights.astype(BF16), preferred_element_type=F32)

    def finish(axis, place, own, summed):
        result = (summed[0:24] / summed[24:25]).astype(BF16)
        back_send[axis, 2 * place] = result[:, :128]
        back_send[axis, 2 * place + 1] = result[:, 128:]
        for peer in [2 * place + 1 - lax.rem(me[axis], 2)] if own else [2 * place, 2 * place + 1]:
            leave(axis, *back, peer).start()

    def place_of(axis, tile):
        outer, inner = me[axis] // 4, lax.rem(me[axis], 4) // 2
        return lax.rem(outer + 1 + tile, 4) * 2 + lax.rem(inner + 1 + tile // 4, 2)

    def step(ahead, behind, buffer, highest):
        later = jnp.full((8, 256), -jnp.inf, F32)
        summed = jnp.zeros((32, 256), F32)
        if ahead is not None:
            query = take_queries(ahead[0], place_of(*ahead))
        for chunk in range(2048 // CHUNK):
            if ahead is not None:
                later = score(ahead[0], query, buffer, chunk, later)
            if behind is not None:
                summed = gather(behind[0], 1 - buffer, chunk, highest, summed)
        if behind is not None:
            finish(behind[0], place_of(*behind), isinstance(behind[1], int) and behind[1] == 7, summed)
        return jnp.max(later, 0, keepdims=True)

    def steps(axis, highest):
        def two(trip, highest):
            highest = step((axis, 2 * trip + 1), (axis, 2 * trip), 1, highest)
            return step((axis, 2 * trip + 2), (axis, 2 * trip + 1), 0, highest)

        highest = lax.fori_loop(0, 3, two, highest)
        return step((axis, 7), (axis, 6), 1, highest)

    take_keys(0)
    all_of(0, *queries).wait_recv()
    highest = step((0, 0), None, 0, None)
    for peer in peers[1]:
        leave(1, *queries, peer).start()
    highest = steps(0, highest)
    take_keys(1)
    all_of(1, *queries).wait_recv()
    highest = step((1, 0), (0, 7), 0, highest)
    highest = steps(1, highest)
    step(None, (1, 7), 0, highest)
    for axis in range(2):
        back_recv[axis, me[axis]] = back_send[axis, me[axis]]

    def mix(axis):
        outs = []
        for stripe in range(2):
            heads = [back_recv[axis, 8 * stripe + head].astype(F32) for head in range(8)]
            mixed = jnp.concatenate(heads, 0).T.astype(BF16)
            outs.append(jnp.dot(mixed, proj_w[axis * HALF : axis * HALF + HALF, :], preferred_element_type=F32))
        return jnp.concatenate(outs, 0)

    for axis in range(2):
        all_of(axis, *kv).wait_send()
        all_of(axis, *queries).wait_send()
    all_of(0, *back).wait_send()
    all_of(0, *back).wait_recv()
    total = mix(0) + lanes_in(token_refs, slice(None)) + proj_bias[...][None, :]
    all_of(1, *back).wait_send()
    all_of(1, *back).wait_recv()
    out_ref[...] = (total + by_row(mix(1))).astype(BF16).reshape(16, 16, DIM)


def on_device(image, conv_weight, conv_bias, merge_gain, merge_shift, norm_gain, norm_shift, qkv_weight, proj_weight, proj_bias):
    dma = pltpu.SemaphoreType.DMA
    return pl.pallas_call(
        kernel,
        out_shape=pltpu.VMEM((16, 16, DIM), BF16),
        in_specs=[pl.BlockSpec(memory_space=pltpu.HBM)] * 10,
        out_specs=pl.BlockSpec(memory_space=pltpu.VMEM),
        scratch_shapes=[pltpu.VMEM((DIM,), F32)] * 6
        + [
            pltpu.VMEM((32, 32, 192), BF16),
            pltpu.VMEM((3, 3, 192, DIM), BF16),
            pltpu.VMEM((DIM, 3 * DIM), BF16),
            pltpu.VMEM((DIM, DIM), BF16),
            pltpu.VMEM((2, 34, 40, 128), F32),
            pltpu.VMEM((3, 17, 2, 16, 192), BF16),
            pltpu.VMEM((3 * DIM, DIM), BF16),
            pltpu.VMEM((80, 128), F32),
            pltpu.VMEM((80, 128), F32),
            pltpu.VMEM((32, 192), BF16),
            pltpu.VMEM((32, 192), BF16),
            pltpu.VMEM((32, 192), BF16),
            pltpu.VMEM((16, 192), BF16),
        ]
        + [pltpu.VMEM((TOKENS, 128), F32)] * 9
        + [pltpu.VMEM((2, PEERS, 2 * DEPTH, 128), BF16)] * 2
        + [pltpu.VMEM((2, PEERS, DEPTH, 128), BF16)] * 4
        + [
            pltpu.VMEM((2, 2048, 128), BF16),
            pltpu.VMEM((2, 32, 2048), BF16),
            pltpu.VMEM((2, 2048, 256), F32),
            dma((10,)),
            dma((3,)),
            dma((3,)),
        ]
        + [dma((2,))] * 6,
        compiler_params=pltpu.CompilerParams(
            collective_id=0, has_side_effects=True, vmem_limit_bytes=66000000),
    )(image, conv_weight, qkv_weight, proj_weight, conv_bias, merge_gain, merge_shift, norm_gain, norm_shift, proj_bias)


def solution(mesh):
    return jax.shard_map(
        on_device,
        mesh=mesh,
        in_specs=(P("row", "col", None), P(), P(), P(), P(), P(), P(), P(), P(), P()),
        out_specs=P("row", "col", None),
        check_vma=False,
    )
```

```python
import math

import jax
import jax.numpy as jnp
from jax import lax
from jax.experimental import pallas as pl
from jax.experimental.pallas import tpu as pltpu
from jax.sharding import PartitionSpec as P

HEADS = 16
PEERS = 16
DEPTH = 24
HALF = 192
DIM = 384
TOKENS = 256
CHUNK = 512
F32 = jnp.float32
BF16 = jnp.bfloat16
MESH = pl.DeviceIdType.MESH
FAR_FIRST = (2, 1, 3, 0)


def layer_norm(values, gain, shift):
    center = values - jnp.mean(values, -1, keepdims=True)
    spread = jnp.mean(center * center, -1, keepdims=True)
    return center * lax.rsqrt(spread + 1e-05) * gain + shift


def by_stripe(values):
    pieces = [values[16 * i + 8 * s : 16 * i + 8 * s + 8] for s in range(2) for i in range(16)]
    return jnp.concatenate(pieces, 0)


def by_row(values):
    pieces = [values[128 * s + 8 * i : 128 * s + 8 * i + 8] for i in range(16) for s in range(2)]
    return jnp.concatenate(pieces, 0)


def lanes_in(refs, rows):
    return jnp.concatenate([ref[rows, :] for ref in refs], 1)


def kernel(
    image_hbm, conv_hbm, qkv_hbm, proj_hbm,
    conv_bias_hbm, merge_gain_hbm, merge_shift_hbm, norm_gain_hbm, norm_shift_hbm, proj_bias_hbm,
    out_ref,
    conv_bias, merge_gain, merge_shift, norm_gain, norm_shift, proj_bias,
    image, conv_w, qkv_w, proj_w, padded, phases, qkv_t,
    edge_low, edge_high,
    column, halo_row, halo_col, halo_corner,
    merged_0, merged_1, merged_2, tokens_0, tokens_1, tokens_2, normed_0, normed_1, normed_2,
    send_kv, recv_kv, send_q, recv_q, back_send, back_recv,
    keys, value_t, scores,
    load_sem, halo_send, halo_recv,
    kv_send_sem, kv_recv_sem, q_send_sem, q_recv_sem, back_send_sem, back_recv_sem, pair_sem,
):
    me_r = lax.axis_index("row")
    me_c = lax.axis_index("col")
    me = (me_c, me_r)
    down, up = lax.rem(me_r + 1, PEERS), lax.rem(me_r + PEERS - 1, PEERS)
    right, left = lax.rem(me_c + 1, PEERS), lax.rem(me_c + PEERS - 1, PEERS)
    merged_refs = (merged_0, merged_1, merged_2)
    token_refs = (tokens_0, tokens_1, tokens_2)
    normed_refs = (normed_0, normed_1, normed_2)

    def device(axis, peer):
        return (me_r, peer) if axis == 0 else (peer, me_c)

    loads = [
        pltpu.make_async_copy(source, target, load_sem.at[place])
        for place, (source, target) in enumerate([
            (image_hbm, image), (qkv_hbm, qkv_w), (conv_hbm, conv_w), (conv_bias_hbm, conv_bias),
            (merge_gain_hbm, merge_gain), (merge_shift_hbm, merge_shift), (norm_gain_hbm, norm_gain),
            (norm_shift_hbm, norm_shift), (proj_bias_hbm, proj_bias), (proj_hbm, proj_w)])
    ]
    for load in loads:
        load.start()

    peers = ([], [])
    for axis in range(2):
        block, place = me[axis] // 4, lax.rem(me[axis], 4)
        for outer in FAR_FIRST:
            for inner in FAR_FIRST:
                if outer or inner:
                    if axis == 0:
                        peers[0].append(lax.rem(block + outer, 4) * 4 + lax.rem(place + inner, 4))
                    else:
                        peers[1].append(lax.rem(block + inner, 4) * 4 + lax.rem(place + outer, 4))

    barrier = pltpu.get_barrier_semaphore()
    for step in range(PEERS - 1):
        for axis in (1, 0):
            pl.semaphore_signal(barrier, inc=1, device_id=device(axis, peers[axis][step]), device_id_type=MESH)
    pl.semaphore_signal(barrier, inc=1, device_id=(down, right), device_id_type=MESH)
    pl.semaphore_signal(barrier, inc=1, device_id=(up, left), device_id_type=MESH)

    def pad(rows, cols, values):
        padded[0, rows, cols, :] = values[:, :, 0:128]
        padded[1, rows, cols, 0:64] = values[:, :, 128:192]

    pad(slice(0, 1), slice(0, 40), jnp.zeros((1, 40, 192), F32))
    pad(slice(1, 33), slice(0, 8), jnp.zeros((32, 8, 192), F32))
    value_t[0, 24:32, :] = jnp.ones((8, 2048), BF16)
    value_t[1, 24:32, :] = jnp.ones((8, 2048), BF16)
    loads[0].wait()
    pad(slice(1, 33), slice(8, 40), image[...].astype(F32))
    column[:, 0:128] = padded[0, 1:33, 39:40, :].reshape(32, 128).astype(BF16)
    column[:, 128:192] = padded[1, 1:33, 39:40, 0:64].reshape(32, 64).astype(BF16)
    loads[1].wait()
    qkv_t[...] = qkv_w[...].T

    pl.semaphore_wait(barrier, 2 * (PEERS - 1) + 2)
    halos = [
        pltpu.make_async_remote_copy(
            src_ref=image.at[31], dst_ref=halo_row, send_sem=halo_send.at[0], recv_sem=halo_recv.at[0],
            device_id=(down, me_c), device_id_type=MESH),
        pltpu.make_async_remote_copy(
            src_ref=column, dst_ref=halo_col, send_sem=halo_send.at[1], recv_sem=halo_recv.at[1],
            device_id=(me_r, right), device_id_type=MESH),
        pltpu.make_async_remote_copy(
            src_ref=column.at[pl.ds(16, 16)], dst_ref=halo_corner, send_sem=halo_send.at[2], recv_sem=halo_recv.at[2],
            device_id=(down, right), device_id_type=MESH),
    ]
    for halo in halos:
        halo.start()

    for load in loads[2:]:
        load.wait()
    for tap in range(3):
        low = padded[0, :, pl.ds(7 + tap, 16, stride=2), :].astype(BF16)
        high = padded[1, :, pl.ds(7 + tap, 16, stride=2), :].astype(BF16)
        phases[tap, :, :, :, 0:128] = low.reshape(17, 2, 16, 128)
        phases[tap, :, :, :, 128:192] = high[:, :, 0:64].reshape(17, 2, 16, 64)
    merged = jnp.zeros((TOKENS, DIM), F32)
    for a in range(3):
        for b in range(3):
            window = phases[b, pl.ds(a // 2, 16), a % 2].reshape(TOKENS, 192)
            merged = merged + jnp.dot(window, conv_w[a, b], preferred_element_type=F32)

    def norms(values):
        merge_affine = merge_gain[...][None, :], merge_shift[...][None, :]
        tokens = layer_norm(values + conv_bias[...][None, :], *merge_affine).astype(BF16).astype(F32)
        return tokens, layer_norm(tokens, norm_gain[...][None, :], norm_shift[...][None, :])

    def keep(refs, rows, values):
        for place, ref in enumerate(refs):
            ref[rows, :] = values[:, 128 * place : 128 * place + 128]

    tokens, normed = norms(merged)
    keep(merged_refs, slice(None), merged)
    keep(token_refs, slice(None), tokens)
    keep(normed_refs, slice(None), normed)

    has_up, has_left = me_r > 0, me_c > 0
    upper, side = slice(0, 16), pl.ds(0, 16, stride=16)

    def edge_store(rows, values):
        edge_low[rows, :] = values[:, 0:128]
        edge_high[rows, 0:64] = values[:, 128:192]

    def edge_load(start):
        rows = pl.ds(start, 16, stride=2)
        return jnp.concatenate([edge_low[rows, :], edge_high[rows, :][:, 0:64]], 1).astype(BF16)

    def left_edge():
        halos[1].wait()
        edge_store(slice(47, 48), jnp.zeros((1, 192), F32))
        edge_store(slice(48, 80), jnp.where(has_left, halo_col[...].astype(F32), 0.0))
        fix = jnp.zeros((16, DIM), F32)
        for tap in range(3):
            fix = fix + jnp.dot(edge_load(47 + tap), conv_w[tap, 0], preferred_element_type=F32)
        fixed = lanes_in(merged_refs, side) + fix
        keep(merged_refs, side, fixed)
        tokens, normed = norms(fixed)
        keep(token_refs, side, tokens)
        keep(normed_refs, side, normed)

    def upper_edge():
        halos[0].wait()
        halos[2].wait()
        corner = jnp.where(jnp.logical_and(has_up, has_left), halo_corner[...].astype(F32)[15:16], 0.0)
        edge_store(slice(7, 8), corner)
        edge_store(slice(8, 40), jnp.where(has_up, halo_row[...].astype(F32), 0.0))
        fixed = lanes_in(merged_refs, upper)
        for tap in range(3):
            fixed = fixed + jnp.dot(edge_load(7 + tap), conv_w[0, tap], preferred_element_type=F32)
        tokens, normed = norms(fixed)
        keep(token_refs, upper, tokens)
        keep(normed_refs, upper, normed)

    def leave_query(peer):
        return pltpu.make_async_remote_copy(
            src_ref=send_q.at[0, peer], dst_ref=recv_q.at[0, me_c],
            send_sem=q_send_sem.at[0], recv_sem=pair_sem.at[me_c // 2],
            device_id=(me_r, peer), device_id_type=MESH)

    def wait_queries(place, count):
        several = pl.ds(0, count)
        pltpu.make_async_remote_copy(
            src_ref=send_q.at[0, several], dst_ref=recv_q.at[0, several],
            send_sem=q_send_sem.at[0], recv_sem=pair_sem.at[place],
            device_id=(me_r, peers[0][0]), device_id_type=MESH).wait_recv()

    def project(values, base, part):
        rows = slice(part * DIM + base, part * DIM + base + HALF)
        return lax.dot_general(qkv_t[rows, :], values, (((1,), (1,)), ((), ())), preferred_element_type=F32)

    def leave(axis, send, recv, sends, recvs, peer):
        return pltpu.make_async_remote_copy(
            src_ref=send.at[axis, peer], dst_ref=recv.at[axis, me[axis]],
            send_sem=sends.at[axis], recv_sem=recvs.at[axis],
            device_id=device(axis, peer), device_id_type=MESH)

    def all_of(axis, send, recv, sends, recvs):
        most = pl.ds(0, PEERS - 1)
        return pltpu.make_async_remote_copy(
            src_ref=send.at[axis, most], dst_ref=recv.at[axis, most],
            send_sem=sends.at[axis], recv_sem=recvs.at[axis],
            device_id=device(axis, peers[axis][0]), device_id_type=MESH)

    kv = (send_kv, recv_kv, kv_send_sem, kv_recv_sem)
    queries = (send_q, recv_q, q_send_sem, q_recv_sem)
    back = (back_send, back_recv, back_send_sem, back_recv_sem)

    def to_stripe(stripe, copy_to):
        for head in range(HEADS // 2):
            peer = 8 * stripe + lax.rem(me_c + 4 + head, 8)

            @pl.when(peer != me_c)
            def _():
                copy_to(peer).start()

    for stripe in (1, 0):
        if stripe:
            left_edge()
        else:
            upper_edge()
        values = lanes_in(normed_refs, slice(128 * stripe, 128 * stripe + 128)).astype(BF16)
        key_part, value_part = (project(values, 0, part) for part in (1, 2))
        for head in range(HEADS // 2):
            rows = slice(DEPTH * head, DEPTH * head + DEPTH)
            block = jnp.concatenate([key_part[rows], value_part[rows]], 0).astype(BF16)
            send_kv[0, 8 * stripe + head] = block
        to_stripe(stripe, lambda peer: leave(0, *kv, peer))
        query_part = project(values, 0, 0)
        for head in range(HEADS // 2):
            send_q[0, 8 * stripe + head] = query_part[DEPTH * head : DEPTH * head + DEPTH].astype(BF16)
        to_stripe(stripe, leave_query)

    values = by_stripe(lanes_in(normed_refs, slice(None))).astype(BF16)
    key_part, value_part = (project(values, HALF, part) for part in (1, 2))
    for head in range(HEADS // 2):
        rows = slice(DEPTH * head, DEPTH * head + DEPTH)
        block = jnp.concatenate([key_part[rows], value_part[rows]], 0).astype(BF16)
        send_kv[1, head] = block[:, :128]
        send_kv[1, 8 + head] = block[:, 128:]
    for peer in peers[1]:
        leave(1, *kv, peer).start()
    query_part = project(values, HALF, 0)
    for head in range(HEADS // 2):
        block = query_part[DEPTH * head : DEPTH * head + DEPTH].astype(BF16)
        send_q[1, head] = block[:, :128]
        send_q[1, 8 + head] = block[:, 128:]
    for axis in range(2):
        recv_kv[axis, me[axis]] = send_kv[axis, me[axis]]
        recv_q[axis, me[axis]] = send_q[axis, me[axis]]

    def take_keys(axis):
        for peer in range(PEERS):
            rows = slice(128 * peer, 128 * peer + 128)
            block = recv_kv[axis, peer]
            value_t[axis, 0:24, rows] = block[24:48]
            own = jnp.concatenate([block.astype(F32)[0:24], jnp.zeros((104, 128), F32)], 0)
            keys[axis, rows, :] = own.T.astype(BF16)

    def take_queries(axis, place):
        pair = [2 * place, 2 * place + 1]
        return jnp.concatenate([recv_q[axis, peer] for peer in pair], 1)

    def score(axis, query, buffer, chunk, highest):
        rows = slice(CHUNK * chunk, CHUNK * chunk + CHUNK)
        part = jnp.dot(keys[axis, rows, 0:24], query, preferred_element_type=F32)
        scores[buffer, rows, :] = part
        return jnp.maximum(highest, jnp.max(part.reshape(CHUNK // 8, 8, 256), 0))

    def gather(axis, buffer, chunk, highest, summed):
        rows = slice(CHUNK * chunk, CHUNK * chunk + CHUNK)
        weights = jnp.exp2((scores[buffer, rows, :] - highest) * (math.log2(math.e) / math.sqrt(DEPTH)))
        return summed + jnp.dot(value_t[axis, :, rows], weights.astype(BF16), preferred_element_type=F32)

    def finish(axis, place, own, summed):
        result = (summed[0:24] / summed[24:25]).astype(BF16)
        back_send[axis, 2 * place] = result[:, :128]
        back_send[axis, 2 * place + 1] = result[:, 128:]
        for peer in [2 * place + 1 - lax.rem(me[axis], 2)] if own else [2 * place, 2 * place + 1]:
            leave(axis, *back, peer).start()

    def place_of(axis, tile):
        outer, inner = me[axis] // 4, lax.rem(me[axis], 4) // 2
        return lax.rem(outer + axis + tile, 4) * 2 + lax.rem(inner + axis + tile // 4, 2)

    def is_own(axis, tile):
        return isinstance(tile, int) and tile == 7 * axis

    def step(ahead, behind, buffer, highest):
        later = jnp.full((8, 256), -jnp.inf, F32)
        summed = jnp.zeros((32, 256), F32)
        if ahead is not None:
            if ahead[0] == 0:
                wait_queries(place_of(*ahead), 1 if is_own(*ahead) else 2)
            query = take_queries(ahead[0], place_of(*ahead))
        for chunk in range(2048 // CHUNK):
            if ahead is not None:
                later = score(ahead[0], query, buffer, chunk, later)
            if behind is not None:
                summed = gather(behind[0], 1 - buffer, chunk, highest, summed)
        if behind is not None:
            finish(behind[0], place_of(*behind), is_own(*behind), summed)
        return jnp.max(later, 0, keepdims=True)

    def steps(axis, initial, highest):
        def two(trip, highest):
            tile = initial + 2 * trip
            highest = step((axis, tile), (axis, tile - 1), initial % 2, highest)
            return step((axis, tile + 1), (axis, tile), 1 - initial % 2, highest)

        return lax.fori_loop(0, 3, two, highest)

    all_of(0, *kv).wait_recv()
    for peer in peers[1]:
        leave(1, *queries, peer).start()
    take_keys(0)
    highest = step((0, 0), None, 0, None)
    highest = step((0, 1), (0, 0), 1, highest)
    highest = steps(0, 2, highest)
    all_of(1, *kv).wait_recv()
    take_keys(1)
    all_of(1, *queries).wait_recv()
    highest = step((1, 0), (0, 7), 0, highest)
    highest = steps(1, 1, highest)
    highest = step((1, 7), (1, 6), 1, highest)
    step(None, (1, 7), 0, highest)
    for axis in range(2):
        back_recv[axis, me[axis]] = back_send[axis, me[axis]]

    def mix(axis):
        outs = []
        for stripe in range(2):
            heads = [back_recv[axis, 8 * stripe + head].astype(F32) for head in range(8)]
            mixed = jnp.concatenate(heads, 0).T.astype(BF16)
            outs.append(jnp.dot(mixed, proj_w[axis * HALF : axis * HALF + HALF, :], preferred_element_type=F32))
        return jnp.concatenate(outs, 0)

    for axis in range(2):
        all_of(axis, *kv).wait_send()
        all_of(axis, *queries).wait_send()
    all_of(0, *back).wait_send()
    all_of(0, *back).wait_recv()
    total = mix(0) + lanes_in(token_refs, slice(None)) + proj_bias[...][None, :]
    all_of(1, *back).wait_send()
    all_of(1, *back).wait_recv()
    out_ref[...] = (total + by_row(mix(1))).astype(BF16).reshape(16, 16, DIM)


def on_device(image, conv_weight, conv_bias, merge_gain, merge_shift, norm_gain, norm_shift, qkv_weight, proj_weight, proj_bias):
    dma = pltpu.SemaphoreType.DMA
    return pl.pallas_call(
        kernel,
        out_shape=pltpu.VMEM((16, 16, DIM), BF16),
        in_specs=[pl.BlockSpec(memory_space=pltpu.HBM)] * 10,
        out_specs=pl.BlockSpec(memory_space=pltpu.VMEM),
        scratch_shapes=[pltpu.VMEM((DIM,), F32)] * 6
        + [
            pltpu.VMEM((32, 32, 192), BF16),
            pltpu.VMEM((3, 3, 192, DIM), BF16),
            pltpu.VMEM((DIM, 3 * DIM), BF16),
            pltpu.VMEM((DIM, DIM), BF16),
            pltpu.VMEM((2, 34, 40, 128), F32),
            pltpu.VMEM((3, 17, 2, 16, 192), BF16),
            pltpu.VMEM((3 * DIM, DIM), BF16),
            pltpu.VMEM((80, 128), F32),
            pltpu.VMEM((80, 128), F32),
            pltpu.VMEM((32, 192), BF16),
            pltpu.VMEM((32, 192), BF16),
            pltpu.VMEM((32, 192), BF16),
            pltpu.VMEM((16, 192), BF16),
        ]
        + [pltpu.VMEM((TOKENS, 128), F32)] * 9
        + [pltpu.VMEM((2, PEERS, 2 * DEPTH, 128), BF16)] * 2
        + [pltpu.VMEM((2, PEERS, DEPTH, 128), BF16)] * 4
        + [
            pltpu.VMEM((2, 2048, 128), BF16),
            pltpu.VMEM((2, 32, 2048), BF16),
            pltpu.VMEM((2, 2048, 256), F32),
            dma((10,)),
            dma((3,)),
            dma((3,)),
        ]
        + [dma((2,))] * 6
        + [dma((PEERS // 2,))],
        compiler_params=pltpu.CompilerParams(
            collective_id=0, has_side_effects=True, vmem_limit_bytes=66000000),
    )(image, conv_weight, qkv_weight, proj_weight, conv_bias, merge_gain, merge_shift, norm_gain, norm_shift, proj_bias)


def solution(mesh):
    return jax.shard_map(
        on_device,
        mesh=mesh,
        in_specs=(P("row", "col", None), P(), P(), P(), P(), P(), P(), P(), P(), P()),
        out_specs=P("row", "col", None),
        check_vma=False,
    )
```

```python
import math

import jax
import jax.numpy as jnp
from jax import lax
from jax.experimental import pallas as pl
from jax.experimental.pallas import tpu as pltpu
from jax.sharding import PartitionSpec as P

HEADS = 16
PEERS = 16
DEPTH = 24
HALF = 192
DIM = 384
TOKENS = 256
CHUNK = 512
F32 = jnp.float32
BF16 = jnp.bfloat16
MESH = pl.DeviceIdType.MESH
FAR_FIRST = (2, 1, 3, 0)


def layer_norm(values, gain, shift):
    center = values - jnp.mean(values, -1, keepdims=True)
    spread = jnp.mean(center * center, -1, keepdims=True)
    return center * lax.rsqrt(spread + 1e-05) * gain + shift


def by_stripe(values):
    pieces = [values[16 * i + 8 * s : 16 * i + 8 * s + 8] for s in range(2) for i in range(16)]
    return jnp.concatenate(pieces, 0)


def by_row(values):
    pieces = [values[128 * s + 8 * i : 128 * s + 8 * i + 8] for i in range(16) for s in range(2)]
    return jnp.concatenate(pieces, 0)


def lanes_in(refs, rows):
    return jnp.concatenate([ref[rows, :] for ref in refs], 1)


def kernel(
    image_hbm, conv_hbm, qkv_hbm, proj_hbm,
    conv_bias_hbm, merge_gain_hbm, merge_shift_hbm, norm_gain_hbm, norm_shift_hbm, proj_bias_hbm,
    out_ref,
    conv_bias, merge_gain, merge_shift, norm_gain, norm_shift, proj_bias,
    image, conv_w, qkv_w, proj_w, padded, phases, qkv_t,
    edge_low, edge_high,
    column, halo_row, halo_col, halo_corner,
    merged_0, merged_1, merged_2, tokens_0, tokens_1, tokens_2, normed_0, normed_1, normed_2,
    send_kv, recv_kv, send_q, recv_q, back_send, back_recv,
    keys, value_t, scores,
    load_sem, halo_send, halo_recv,
    kv_send_sem, kv_recv_sem, q_send_sem, q_recv_sem, back_send_sem, back_recv_sem, pair_sem,
):
    me_r = lax.axis_index("row")
    me_c = lax.axis_index("col")
    me = (me_c, me_r)
    down, up = lax.rem(me_r + 1, PEERS), lax.rem(me_r + PEERS - 1, PEERS)
    right, left = lax.rem(me_c + 1, PEERS), lax.rem(me_c + PEERS - 1, PEERS)
    merged_refs = (merged_0, merged_1, merged_2)
    token_refs = (tokens_0, tokens_1, tokens_2)
    normed_refs = (normed_0, normed_1, normed_2)

    def device(axis, peer):
        return (me_r, peer) if axis == 0 else (peer, me_c)

    loads = [
        pltpu.make_async_copy(source, target, load_sem.at[place])
        for place, (source, target) in enumerate([
            (image_hbm, image), (qkv_hbm, qkv_w), (conv_hbm, conv_w), (conv_bias_hbm, conv_bias),
            (merge_gain_hbm, merge_gain), (merge_shift_hbm, merge_shift), (norm_gain_hbm, norm_gain),
            (norm_shift_hbm, norm_shift), (proj_bias_hbm, proj_bias), (proj_hbm, proj_w)])
    ]
    for load in loads:
        load.start()

    peers = ([], [])
    for axis in range(2):
        block, place = me[axis] // 4, lax.rem(me[axis], 4)
        for outer in FAR_FIRST:
            for inner in FAR_FIRST:
                if outer or inner:
                    if axis == 0:
                        peers[0].append(lax.rem(block + outer, 4) * 4 + lax.rem(place + inner, 4))
                    else:
                        peers[1].append(lax.rem(block + inner, 4) * 4 + lax.rem(place + outer, 4))

    barrier = pltpu.get_barrier_semaphore()
    for step in range(PEERS - 1):
        for axis in (1, 0):
            pl.semaphore_signal(barrier, inc=1, device_id=device(axis, peers[axis][step]), device_id_type=MESH)
    pl.semaphore_signal(barrier, inc=1, device_id=(down, right), device_id_type=MESH)
    pl.semaphore_signal(barrier, inc=1, device_id=(up, left), device_id_type=MESH)

    def pad(rows, cols, values):
        padded[0, rows, cols, :] = values[:, :, 0:128]
        padded[1, rows, cols, 0:64] = values[:, :, 128:192]

    pad(slice(0, 1), slice(0, 40), jnp.zeros((1, 40, 192), F32))
    pad(slice(1, 33), slice(0, 8), jnp.zeros((32, 8, 192), F32))
    value_t[0, 24:32, :] = jnp.ones((8, 2048), BF16)
    value_t[1, 24:32, :] = jnp.ones((8, 2048), BF16)
    loads[0].wait()
    pad(slice(1, 33), slice(8, 40), image[...].astype(F32))
    column[:, 0:128] = padded[0, 1:33, 39:40, :].reshape(32, 128).astype(BF16)
    column[:, 128:192] = padded[1, 1:33, 39:40, 0:64].reshape(32, 64).astype(BF16)
    loads[1].wait()
    qkv_t[...] = qkv_w[...].T

    pl.semaphore_wait(barrier, 2 * (PEERS - 1) + 2)
    halos = [
        pltpu.make_async_remote_copy(
            src_ref=image.at[31], dst_ref=halo_row, send_sem=halo_send.at[0], recv_sem=halo_recv.at[0],
            device_id=(down, me_c), device_id_type=MESH),
        pltpu.make_async_remote_copy(
            src_ref=column, dst_ref=halo_col, send_sem=halo_send.at[1], recv_sem=halo_recv.at[1],
            device_id=(me_r, right), device_id_type=MESH),
        pltpu.make_async_remote_copy(
            src_ref=column.at[pl.ds(16, 16)], dst_ref=halo_corner, send_sem=halo_send.at[2], recv_sem=halo_recv.at[2],
            device_id=(down, right), device_id_type=MESH),
    ]
    for halo in halos:
        halo.start()

    for load in loads[2:]:
        load.wait()
    for tap in range(3):
        low = padded[0, :, pl.ds(7 + tap, 16, stride=2), :].astype(BF16)
        high = padded[1, :, pl.ds(7 + tap, 16, stride=2), :].astype(BF16)
        phases[tap, :, :, :, 0:128] = low.reshape(17, 2, 16, 128)
        phases[tap, :, :, :, 128:192] = high[:, :, 0:64].reshape(17, 2, 16, 64)
    merged = jnp.zeros((TOKENS, DIM), F32)
    for a in range(3):
        for b in range(3):
            window = phases[b, pl.ds(a // 2, 16), a % 2].reshape(TOKENS, 192)
            merged = merged + jnp.dot(window, conv_w[a, b], preferred_element_type=F32)

    def norms(values):
        merge_affine = merge_gain[...][None, :], merge_shift[...][None, :]
        tokens = layer_norm(values + conv_bias[...][None, :], *merge_affine).astype(BF16).astype(F32)
        return tokens, layer_norm(tokens, norm_gain[...][None, :], norm_shift[...][None, :])

    def keep(refs, rows, values):
        for place, ref in enumerate(refs):
            ref[rows, :] = values[:, 128 * place : 128 * place + 128]

    tokens, normed = norms(merged)
    keep(merged_refs, slice(None), merged)
    keep(token_refs, slice(None), tokens)
    keep(normed_refs, slice(None), normed)

    has_up, has_left = me_r > 0, me_c > 0
    upper, side = slice(0, 16), pl.ds(0, 16, stride=16)

    def edge_store(rows, values):
        edge_low[rows, :] = values[:, 0:128]
        edge_high[rows, 0:64] = values[:, 128:192]

    def edge_load(start):
        rows = pl.ds(start, 16, stride=2)
        return jnp.concatenate([edge_low[rows, :], edge_high[rows, :][:, 0:64]], 1).astype(BF16)

    def left_edge():
        halos[1].wait()
        edge_store(slice(47, 48), jnp.zeros((1, 192), F32))
        edge_store(slice(48, 80), jnp.where(has_left, halo_col[...].astype(F32), 0.0))
        fix = jnp.zeros((16, DIM), F32)
        for tap in range(3):
            fix = fix + jnp.dot(edge_load(47 + tap), conv_w[tap, 0], preferred_element_type=F32)
        fixed = lanes_in(merged_refs, side) + fix
        keep(merged_refs, side, fixed)
        tokens, normed = norms(fixed)
        keep(token_refs, side, tokens)
        keep(normed_refs, side, normed)

    def upper_edge():
        halos[0].wait()
        halos[2].wait()
        corner = jnp.where(jnp.logical_and(has_up, has_left), halo_corner[...].astype(F32)[15:16], 0.0)
        edge_store(slice(7, 8), corner)
        edge_store(slice(8, 40), jnp.where(has_up, halo_row[...].astype(F32), 0.0))
        fixed = lanes_in(merged_refs, upper)
        for tap in range(3):
            fixed = fixed + jnp.dot(edge_load(7 + tap), conv_w[0, tap], preferred_element_type=F32)
        tokens, normed = norms(fixed)
        keep(token_refs, upper, tokens)
        keep(normed_refs, upper, normed)

    def leave_query(peer):
        return pltpu.make_async_remote_copy(
            src_ref=send_q.at[0, peer], dst_ref=recv_q.at[0, me_c],
            send_sem=q_send_sem.at[0], recv_sem=pair_sem.at[me_c // 2],
            device_id=(me_r, peer), device_id_type=MESH)

    def wait_queries(place, count):
        several = pl.ds(0, count)
        pltpu.make_async_remote_copy(
            src_ref=send_q.at[0, several], dst_ref=recv_q.at[0, several],
            send_sem=q_send_sem.at[0], recv_sem=pair_sem.at[place],
            device_id=(me_r, peers[0][0]), device_id_type=MESH).wait_recv()

    def project(values, base, part):
        rows = slice(part * DIM + base, part * DIM + base + HALF)
        return lax.dot_general(qkv_t[rows, :], values, (((1,), (1,)), ((), ())), preferred_element_type=F32)

    def leave(axis, send, recv, sends, recvs, peer):
        return pltpu.make_async_remote_copy(
            src_ref=send.at[axis, peer], dst_ref=recv.at[axis, me[axis]],
            send_sem=sends.at[axis], recv_sem=recvs.at[axis],
            device_id=device(axis, peer), device_id_type=MESH)

    def all_of(axis, send, recv, sends, recvs):
        most = pl.ds(0, PEERS - 1)
        return pltpu.make_async_remote_copy(
            src_ref=send.at[axis, most], dst_ref=recv.at[axis, most],
            send_sem=sends.at[axis], recv_sem=recvs.at[axis],
            device_id=device(axis, peers[axis][0]), device_id_type=MESH)

    kv = (send_kv, recv_kv, kv_send_sem, kv_recv_sem)
    queries = (send_q, recv_q, q_send_sem, q_recv_sem)
    back = (back_send, back_recv, back_send_sem, back_recv_sem)

    def to_stripe(stripe, copy_to):
        for head in range(HEADS // 2):
            peer = 8 * stripe + lax.rem(me_c + 4 + head, 8)

            @pl.when(peer != me_c)
            def _():
                copy_to(peer).start()

    for stripe in (1, 0):
        if stripe:
            left_edge()
        else:
            upper_edge()
        values = lanes_in(normed_refs, slice(128 * stripe, 128 * stripe + 128)).astype(BF16)
        key_part, value_part = (project(values, 0, part) for part in (1, 2))
        for head in range(HEADS // 2):
            rows = slice(DEPTH * head, DEPTH * head + DEPTH)
            block = jnp.concatenate([key_part[rows], value_part[rows]], 0).astype(BF16)
            send_kv[0, 8 * stripe + head] = block
        to_stripe(stripe, lambda peer: leave(0, *kv, peer))
        query_part = project(values, 0, 0)
        for head in range(HEADS // 2):
            send_q[0, 8 * stripe + head] = query_part[DEPTH * head : DEPTH * head + DEPTH].astype(BF16)
        to_stripe(stripe, leave_query)

    values = by_stripe(lanes_in(normed_refs, slice(None))).astype(BF16)
    key_part, value_part = (project(values, HALF, part) for part in (1, 2))
    for head in range(HEADS // 2):
        rows = slice(DEPTH * head, DEPTH * head + DEPTH)
        block = jnp.concatenate([key_part[rows], value_part[rows]], 0).astype(BF16)
        send_kv[1, head] = block[:, :128]
        send_kv[1, 8 + head] = block[:, 128:]
    for peer in peers[1]:
        leave(1, *kv, peer).start()
    query_part = project(values, HALF, 0)
    for head in range(HEADS // 2):
        block = query_part[DEPTH * head : DEPTH * head + DEPTH].astype(BF16)
        send_q[1, head] = block[:, :128]
        send_q[1, 8 + head] = block[:, 128:]
    for axis in range(2):
        recv_kv[axis, me[axis]] = send_kv[axis, me[axis]]
        recv_q[axis, me[axis]] = send_q[axis, me[axis]]

    def take_keys(axis):
        for peer in range(PEERS):
            rows = slice(128 * peer, 128 * peer + 128)
            block = recv_kv[axis, peer]
            value_t[axis, 0:24, rows] = block[24:48]
            own = jnp.concatenate([block.astype(F32)[0:24], jnp.zeros((104, 128), F32)], 0)
            keys[axis, rows, :] = own.T.astype(BF16)

    def take_queries(axis, place):
        pair = [2 * place, 2 * place + 1]
        return jnp.concatenate([recv_q[axis, peer] for peer in pair], 1)

    def score(axis, query, buffer, chunk, highest):
        rows = slice(CHUNK * chunk, CHUNK * chunk + CHUNK)
        part = jnp.dot(keys[axis, rows, 0:24], query, preferred_element_type=F32)
        scores[buffer, rows, :] = part
        return jnp.maximum(highest, jnp.max(part.reshape(CHUNK // 8, 8, 256), 0))

    def gather(axis, buffer, chunk, highest, summed):
        rows = slice(CHUNK * chunk, CHUNK * chunk + CHUNK)
        weights = jnp.exp2((scores[buffer, rows, :] - highest) * (math.log2(math.e) / math.sqrt(DEPTH)))
        return summed + jnp.dot(value_t[axis, :, rows], weights.astype(BF16), preferred_element_type=F32)

    def finish(axis, place, own, summed):
        result = (summed[0:24] / summed[24:25]).astype(BF16)
        back_send[axis, 2 * place] = result[:, :128]
        back_send[axis, 2 * place + 1] = result[:, 128:]
        for peer in [2 * place + 1 - lax.rem(me[axis], 2)] if own else [2 * place, 2 * place + 1]:
            leave(axis, *back, peer).start()

    def place_of(axis, tile):
        outer, inner = me[axis] // 4, lax.rem(me[axis], 4) // 2
        return lax.rem(outer + axis + tile, 4) * 2 + lax.rem(inner + axis + tile // 4, 2)

    def is_own(axis, tile):
        return isinstance(tile, int) and tile == 7 * axis

    def step(ahead, behind, buffer, highest):
        later = jnp.full((8, 256), -jnp.inf, F32)
        summed = jnp.zeros((32, 256), F32)
        if ahead is not None:
            if ahead[0] == 0:
                wait_queries(place_of(*ahead), 1 if is_own(*ahead) else 2)
            query = take_queries(ahead[0], place_of(*ahead))
        for chunk in range(2048 // CHUNK):
            if ahead is not None:
                later = score(ahead[0], query, buffer, chunk, later)
            if behind is not None:
                summed = gather(behind[0], 1 - buffer, chunk, highest, summed)
        if behind is not None:
            finish(behind[0], place_of(*behind), is_own(*behind), summed)
        return jnp.max(later, 0, keepdims=True)

    def steps(axis, initial, highest):
        def two(trip, highest):
            tile = initial + 2 * trip
            highest = step((axis, tile), (axis, tile - 1), initial % 2, highest)
            return step((axis, tile + 1), (axis, tile), 1 - initial % 2, highest)

        return lax.fori_loop(0, 3, two, highest)

    all_of(0, *kv).wait_recv()
    for peer in peers[1]:
        leave(1, *queries, peer).start()
    take_keys(0)
    highest = step((0, 0), None, 0, None)
    highest = step((0, 1), (0, 0), 1, highest)
    highest = steps(0, 2, highest)
    all_of(1, *kv).wait_recv()
    take_keys(1)
    all_of(1, *queries).wait_recv()
    highest = step((1, 0), (0, 7), 0, highest)
    highest = steps(1, 1, highest)
    highest = step((1, 7), (1, 6), 1, highest)
    step(None, (1, 7), 0, highest)
    for axis in range(2):
        back_recv[axis, me[axis]] = back_send[axis, me[axis]]

    def mix(axis):
        outs = []
        for stripe in range(2):
            heads = [back_recv[axis, 8 * stripe + head].astype(F32) for head in range(8)]
            mixed = jnp.concatenate(heads, 0).astype(BF16).T
            outs.append(jnp.dot(mixed, proj_w[axis * HALF : axis * HALF + HALF, :], preferred_element_type=F32))
        return jnp.concatenate(outs, 0)

    for axis in range(2):
        all_of(axis, *kv).wait_send()
        all_of(axis, *queries).wait_send()
    all_of(0, *back).wait_send()
    all_of(0, *back).wait_recv()
    total = mix(0) + lanes_in(token_refs, slice(None)) + proj_bias[...][None, :]
    all_of(1, *back).wait_send()
    all_of(1, *back).wait_recv()
    out_ref[...] = (total + by_row(mix(1))).astype(BF16).reshape(16, 16, DIM)


def on_device(image, conv_weight, conv_bias, merge_gain, merge_shift, norm_gain, norm_shift, qkv_weight, proj_weight, proj_bias):
    dma = pltpu.SemaphoreType.DMA
    return pl.pallas_call(
        kernel,
        out_shape=pltpu.VMEM((16, 16, DIM), BF16),
        in_specs=[pl.BlockSpec(memory_space=pltpu.HBM)] * 10,
        out_specs=pl.BlockSpec(memory_space=pltpu.VMEM),
        scratch_shapes=[pltpu.VMEM((DIM,), F32)] * 6
        + [
            pltpu.VMEM((32, 32, 192), BF16),
            pltpu.VMEM((3, 3, 192, DIM), BF16),
            pltpu.VMEM((DIM, 3 * DIM), BF16),
            pltpu.VMEM((DIM, DIM), BF16),
            pltpu.VMEM((2, 34, 40, 128), F32),
            pltpu.VMEM((3, 17, 2, 16, 192), BF16),
            pltpu.VMEM((3 * DIM, DIM), BF16),
            pltpu.VMEM((80, 128), F32),
            pltpu.VMEM((80, 128), F32),
            pltpu.VMEM((32, 192), BF16),
            pltpu.VMEM((32, 192), BF16),
            pltpu.VMEM((32, 192), BF16),
            pltpu.VMEM((16, 192), BF16),
        ]
        + [pltpu.VMEM((TOKENS, 128), F32)] * 9
        + [pltpu.VMEM((2, PEERS, 2 * DEPTH, 128), BF16)] * 2
        + [pltpu.VMEM((2, PEERS, DEPTH, 128), BF16)] * 4
        + [
            pltpu.VMEM((2, 2048, 128), BF16),
            pltpu.VMEM((2, 32, 2048), BF16),
            pltpu.VMEM((2, 2048, 256), F32),
            dma((10,)),
            dma((3,)),
            dma((3,)),
        ]
        + [dma((2,))] * 6
        + [dma((PEERS // 2,))],
        compiler_params=pltpu.CompilerParams(
            collective_id=0, has_side_effects=True, vmem_limit_bytes=66000000),
    )(image, conv_weight, qkv_weight, proj_weight, conv_bias, merge_gain, merge_shift, norm_gain, norm_shift, proj_bias)


def solution(mesh):
    return jax.shard_map(
        on_device,
        mesh=mesh,
        in_specs=(P("row", "col", None), P(), P(), P(), P(), P(), P(), P(), P(), P()),
        out_specs=P("row", "col", None),
        check_vma=False,
    )
```

```python
import math

import jax
import jax.numpy as jnp
from jax import lax
from jax.experimental import pallas as pl
from jax.experimental.pallas import tpu as pltpu
from jax.sharding import PartitionSpec as P

HEADS = 16
PEERS = 16
DEPTH = 24
HALF = 192
DIM = 384
TOKENS = 256
CHUNK = 512
F32 = jnp.float32
BF16 = jnp.bfloat16
MESH = pl.DeviceIdType.MESH
FAR_FIRST = (2, 1, 3, 0)


def layer_norm(values, gain, shift):
    center = values - jnp.mean(values, -1, keepdims=True)
    spread = jnp.mean(center * center, -1, keepdims=True)
    return center * lax.rsqrt(spread + 1e-05) * gain + shift


def by_stripe(values):
    pieces = [values[16 * i + 8 * s : 16 * i + 8 * s + 8] for s in range(2) for i in range(16)]
    return jnp.concatenate(pieces, 0)


def by_row(values):
    pieces = [values[128 * s + 8 * i : 128 * s + 8 * i + 8] for i in range(16) for s in range(2)]
    return jnp.concatenate(pieces, 0)


def lanes_in(refs, rows):
    return jnp.concatenate([ref[rows, :] for ref in refs], 1)


def kernel(
    image_hbm, conv_hbm, qkv_hbm, proj_hbm,
    conv_bias_hbm, merge_gain_hbm, merge_shift_hbm, norm_gain_hbm, norm_shift_hbm, proj_bias_hbm,
    out_ref,
    conv_bias, merge_gain, merge_shift, norm_gain, norm_shift, proj_bias,
    image, conv_w, qkv_w, proj_w, padded, phases, qkv_t,
    edge_low, edge_high,
    column, halo_row, halo_col, halo_corner,
    merged_0, merged_1, merged_2, tokens_0, tokens_1, tokens_2, normed_0, normed_1, normed_2,
    send_kv, recv_kv, send_q, recv_q, back_send, back_recv,
    keys, value_t, scores,
    load_sem, halo_send, halo_recv,
    kv_send_sem, kv_recv_sem, q_send_sem, q_recv_sem, back_send_sem, back_recv_sem, pair_sem,
):
    me_r = lax.axis_index("row")
    me_c = lax.axis_index("col")
    me = (me_c, me_r)
    down, up = lax.rem(me_r + 1, PEERS), lax.rem(me_r + PEERS - 1, PEERS)
    right, left = lax.rem(me_c + 1, PEERS), lax.rem(me_c + PEERS - 1, PEERS)
    merged_refs = (merged_0, merged_1, merged_2)
    token_refs = (tokens_0, tokens_1, tokens_2)
    normed_refs = (normed_0, normed_1, normed_2)

    def device(axis, peer):
        return (me_r, peer) if axis == 0 else (peer, me_c)

    loads = [
        pltpu.make_async_copy(source, target, load_sem.at[place])
        for place, (source, target) in enumerate([
            (image_hbm, image), (qkv_hbm, qkv_w), (conv_hbm, conv_w), (conv_bias_hbm, conv_bias),
            (merge_gain_hbm, merge_gain), (merge_shift_hbm, merge_shift), (norm_gain_hbm, norm_gain),
            (norm_shift_hbm, norm_shift), (proj_bias_hbm, proj_bias), (proj_hbm, proj_w)])
    ]
    for load in loads:
        load.start()

    peers = ([], [])
    for axis in range(2):
        block, place = me[axis] // 4, lax.rem(me[axis], 4)
        for outer in FAR_FIRST:
            for inner in FAR_FIRST:
                if outer or inner:
                    if axis == 0:
                        peers[0].append(lax.rem(block + outer, 4) * 4 + lax.rem(place + inner, 4))
                    else:
                        peers[1].append(lax.rem(block + inner, 4) * 4 + lax.rem(place + outer, 4))

    barrier = pltpu.get_barrier_semaphore()
    for step in range(PEERS - 1):
        for axis in (1, 0):
            pl.semaphore_signal(barrier, inc=1, device_id=device(axis, peers[axis][step]), device_id_type=MESH)
    pl.semaphore_signal(barrier, inc=1, device_id=(down, right), device_id_type=MESH)
    pl.semaphore_signal(barrier, inc=1, device_id=(up, left), device_id_type=MESH)

    def pad(rows, cols, values):
        padded[0, rows, cols, :] = values[:, :, 0:128]
        padded[1, rows, cols, 0:64] = values[:, :, 128:192]

    pad(slice(0, 1), slice(0, 40), jnp.zeros((1, 40, 192), F32))
    pad(slice(1, 33), slice(0, 8), jnp.zeros((32, 8, 192), F32))
    value_t[0, 24:32, :] = jnp.ones((8, 2048), BF16)
    value_t[1, 24:32, :] = jnp.ones((8, 2048), BF16)
    loads[0].wait()
    pad(slice(1, 33), slice(8, 40), image[...].astype(F32))
    column[:, 0:128] = padded[0, 1:33, 39:40, :].reshape(32, 128).astype(BF16)
    column[:, 128:192] = padded[1, 1:33, 39:40, 0:64].reshape(32, 64).astype(BF16)
    loads[1].wait()
    qkv_t[...] = qkv_w[...].T

    pl.semaphore_wait(barrier, 2 * (PEERS - 1) + 2)
    halos = [
        pltpu.make_async_remote_copy(
            src_ref=image.at[31], dst_ref=halo_row, send_sem=halo_send.at[0], recv_sem=halo_recv.at[0],
            device_id=(down, me_c), device_id_type=MESH),
        pltpu.make_async_remote_copy(
            src_ref=column, dst_ref=halo_col, send_sem=halo_send.at[1], recv_sem=halo_recv.at[1],
            device_id=(me_r, right), device_id_type=MESH),
        pltpu.make_async_remote_copy(
            src_ref=column.at[pl.ds(16, 16)], dst_ref=halo_corner, send_sem=halo_send.at[2], recv_sem=halo_recv.at[2],
            device_id=(down, right), device_id_type=MESH),
    ]
    for halo in halos:
        halo.start()

    for load in loads[2:]:
        load.wait()
    for tap in range(3):
        low = padded[0, :, pl.ds(7 + tap, 16, stride=2), :].astype(BF16)
        high = padded[1, :, pl.ds(7 + tap, 16, stride=2), :].astype(BF16)
        phases[tap, :, :, :, 0:128] = low.reshape(17, 2, 16, 128)
        phases[tap, :, :, :, 128:192] = high[:, :, 0:64].reshape(17, 2, 16, 64)
    merged = jnp.zeros((TOKENS, DIM), F32)
    for a in range(3):
        for b in range(3):
            window = phases[b, pl.ds(a // 2, 16), a % 2].reshape(TOKENS, 192)
            merged = merged + jnp.dot(window, conv_w[a, b], preferred_element_type=F32)

    def norms(values):
        merge_affine = merge_gain[...][None, :], merge_shift[...][None, :]
        tokens = layer_norm(values + conv_bias[...][None, :], *merge_affine).astype(BF16).astype(F32)
        return tokens, layer_norm(tokens, norm_gain[...][None, :], norm_shift[...][None, :])

    def keep(refs, rows, values):
        for place, ref in enumerate(refs):
            ref[rows, :] = values[:, 128 * place : 128 * place + 128]

    tokens, normed = norms(merged)
    keep(merged_refs, slice(None), merged)
    keep(token_refs, slice(None), tokens)
    keep(normed_refs, slice(None), normed)

    has_up, has_left = me_r > 0, me_c > 0
    upper, side = slice(0, 16), pl.ds(0, 16, stride=16)

    def edge_store(rows, values):
        edge_low[rows, :] = values[:, 0:128]
        edge_high[rows, 0:64] = values[:, 128:192]

    def edge_load(start):
        rows = pl.ds(start, 16, stride=2)
        return jnp.concatenate([edge_low[rows, :], edge_high[rows, :][:, 0:64]], 1).astype(BF16)

    def left_edge():
        halos[1].wait()
        edge_store(slice(47, 48), jnp.zeros((1, 192), F32))
        edge_store(slice(48, 80), jnp.where(has_left, halo_col[...].astype(F32), 0.0))
        fix = jnp.zeros((16, DIM), F32)
        for tap in range(3):
            fix = fix + jnp.dot(edge_load(47 + tap), conv_w[tap, 0], preferred_element_type=F32)
        fixed = lanes_in(merged_refs, side) + fix
        keep(merged_refs, side, fixed)
        tokens, normed = norms(fixed)
        keep(token_refs, side, tokens)
        keep(normed_refs, side, normed)

    def upper_edge():
        halos[0].wait()
        halos[2].wait()
        corner = jnp.where(jnp.logical_and(has_up, has_left), halo_corner[...].astype(F32)[15:16], 0.0)
        edge_store(slice(7, 8), corner)
        edge_store(slice(8, 40), jnp.where(has_up, halo_row[...].astype(F32), 0.0))
        fixed = lanes_in(merged_refs, upper)
        for tap in range(3):
            fixed = fixed + jnp.dot(edge_load(7 + tap), conv_w[0, tap], preferred_element_type=F32)
        tokens, normed = norms(fixed)
        keep(token_refs, upper, tokens)
        keep(normed_refs, upper, normed)

    def leave_query(peer):
        return pltpu.make_async_remote_copy(
            src_ref=send_q.at[0, peer], dst_ref=recv_q.at[0, me_c],
            send_sem=q_send_sem.at[0], recv_sem=pair_sem.at[me_c // 2],
            device_id=(me_r, peer), device_id_type=MESH)

    def wait_queries(place, count):
        several = pl.ds(0, count)
        pltpu.make_async_remote_copy(
            src_ref=send_q.at[0, several], dst_ref=recv_q.at[0, several],
            send_sem=q_send_sem.at[0], recv_sem=pair_sem.at[place],
            device_id=(me_r, peers[0][0]), device_id_type=MESH).wait_recv()

    def project(values, base, part):
        rows = slice(part * DIM + base, part * DIM + base + HALF)
        return lax.dot_general(qkv_t[rows, :], values, (((1,), (1,)), ((), ())), preferred_element_type=F32)

    def leave(axis, send, recv, sends, recvs, peer):
        return pltpu.make_async_remote_copy(
            src_ref=send.at[axis, peer], dst_ref=recv.at[axis, me[axis]],
            send_sem=sends.at[axis], recv_sem=recvs.at[axis],
            device_id=device(axis, peer), device_id_type=MESH)

    def all_of(axis, send, recv, sends, recvs):
        most = pl.ds(0, PEERS - 1)
        return pltpu.make_async_remote_copy(
            src_ref=send.at[axis, most], dst_ref=recv.at[axis, most],
            send_sem=sends.at[axis], recv_sem=recvs.at[axis],
            device_id=device(axis, peers[axis][0]), device_id_type=MESH)

    kv = (send_kv, recv_kv, kv_send_sem, kv_recv_sem)
    queries = (send_q, recv_q, q_send_sem, q_recv_sem)
    back = (back_send, back_recv, back_send_sem, back_recv_sem)

    def to_stripe(stripe, copy_to):
        for head in range(HEADS // 2):
            peer = 8 * stripe + lax.rem(me_c + 4 + head, 8)

            @pl.when(peer != me_c)
            def _():
                copy_to(peer).start()

    for stripe in (1, 0):
        if stripe:
            left_edge()
        else:
            upper_edge()
        values = lanes_in(normed_refs, slice(128 * stripe, 128 * stripe + 128)).astype(BF16)
        key_part, value_part = (project(values, 0, part) for part in (1, 2))
        for head in range(HEADS // 2):
            rows = slice(DEPTH * head, DEPTH * head + DEPTH)
            block = jnp.concatenate([key_part[rows], value_part[rows]], 0).astype(BF16)
            send_kv[0, 8 * stripe + head] = block
        to_stripe(stripe, lambda peer: leave(0, *kv, peer))
        query_part = project(values, 0, 0)
        for head in range(HEADS // 2):
            send_q[0, 8 * stripe + head] = query_part[DEPTH * head : DEPTH * head + DEPTH].astype(BF16)
        to_stripe(stripe, leave_query)

    values = by_stripe(lanes_in(normed_refs, slice(None))).astype(BF16)
    key_part, value_part = (project(values, HALF, part) for part in (1, 2))
    for head in range(HEADS // 2):
        rows = slice(DEPTH * head, DEPTH * head + DEPTH)
        block = jnp.concatenate([key_part[rows], value_part[rows]], 0).astype(BF16)
        send_kv[1, head] = block[:, :128]
        send_kv[1, 8 + head] = block[:, 128:]
    for peer in peers[1]:
        leave(1, *kv, peer).start()
    query_part = project(values, HALF, 0)
    for head in range(HEADS // 2):
        block = query_part[DEPTH * head : DEPTH * head + DEPTH].astype(BF16)
        send_q[1, head] = block[:, :128]
        send_q[1, 8 + head] = block[:, 128:]
    for axis in range(2):
        recv_kv[axis, me[axis]] = send_kv[axis, me[axis]]
        recv_q[axis, me[axis]] = send_q[axis, me[axis]]

    def take_keys(axis):
        for peer in range(PEERS):
            rows = slice(128 * peer, 128 * peer + 128)
            block = recv_kv[axis, peer]
            value_t[axis, 0:24, rows] = block[24:48]
            own = jnp.concatenate([block.astype(F32)[0:24], jnp.zeros((104, 128), F32)], 0)
            keys[axis, rows, :] = own.T.astype(BF16)

    def take_queries(axis, place):
        pair = [2 * place, 2 * place + 1]
        return jnp.concatenate([recv_q[axis, peer] for peer in pair], 1)

    def score(axis, query, buffer, chunk, highest):
        rows = slice(CHUNK * chunk, CHUNK * chunk + CHUNK)
        part = jnp.dot(keys[axis, rows, 0:24], query, preferred_element_type=F32)
        scores[buffer, rows, :] = part
        return jnp.maximum(highest, jnp.max(part.reshape(CHUNK // 8, 8, 256), 0))

    def gather(axis, buffer, chunk, highest, summed):
        rows = slice(CHUNK * chunk, CHUNK * chunk + CHUNK)
        weights = jnp.exp2((scores[buffer, rows, :] - highest) * (math.log2(math.e) / math.sqrt(DEPTH)))
        return summed + jnp.dot(value_t[axis, :, rows], weights.astype(BF16), preferred_element_type=F32)

    def finish(axis, place, own, summed):
        result = (summed[0:24] / summed[24:25]).astype(BF16)
        back_send[axis, 2 * place] = result[:, :128]
        back_send[axis, 2 * place + 1] = result[:, 128:]
        for peer in [2 * place + 1 - lax.rem(me[axis], 2)] if own else [2 * place, 2 * place + 1]:
            leave(axis, *back, peer).start()

    def place_of(axis, tile):
        outer, inner = me[axis] // 4, lax.rem(me[axis], 4) // 2
        return lax.rem(outer + axis + tile, 4) * 2 + lax.rem(inner + axis + tile // 4, 2)

    def is_own(axis, tile):
        return isinstance(tile, int) and tile == 7 * axis

    def step(ahead, behind, buffer, highest):
        later = jnp.full((8, 256), -jnp.inf, F32)
        summed = jnp.zeros((32, 256), F32)
        if ahead is not None:
            if ahead[0] == 0:
                wait_queries(place_of(*ahead), 1 if is_own(*ahead) else 2)
            query = take_queries(ahead[0], place_of(*ahead))
        for chunk in range(2048 // CHUNK):
            if ahead is not None:
                later = score(ahead[0], query, buffer, chunk, later)
            if behind is not None:
                summed = gather(behind[0], 1 - buffer, chunk, highest, summed)
        if behind is not None:
            finish(behind[0], place_of(*behind), is_own(*behind), summed)
        return jnp.max(later, 0, keepdims=True)

    def steps(axis, initial, highest):
        def two(trip, highest):
            tile = initial + 2 * trip
            highest = step((axis, tile), (axis, tile - 1), initial % 2, highest)
            return step((axis, tile + 1), (axis, tile), 1 - initial % 2, highest)

        return lax.fori_loop(0, 3, two, highest)

    all_of(0, *kv).wait_recv()
    for peer in peers[1]:
        leave(1, *queries, peer).start()
    take_keys(0)
    highest = step((0, 0), None, 0, None)
    highest = step((0, 1), (0, 0), 1, highest)
    highest = steps(0, 2, highest)
    all_of(1, *kv).wait_recv()
    take_keys(1)
    all_of(1, *queries).wait_recv()
    highest = step((1, 0), (0, 7), 0, highest)
    highest = steps(1, 1, highest)
    highest = step((1, 7), (1, 6), 1, highest)
    step(None, (1, 7), 0, highest)
    for axis in range(2):
        back_recv[axis, me[axis]] = back_send[axis, me[axis]]

    def mix(axis):
        outs = []
        for stripe in range(2):
            heads = [back_recv[axis, 8 * stripe + head].astype(F32) for head in range(8)]
            mixed = jnp.concatenate(heads, 0).astype(BF16).T
            outs.append(jnp.dot(mixed, proj_w[axis * HALF : axis * HALF + HALF, :], preferred_element_type=F32))
        return jnp.concatenate(outs, 0)

    for axis in range(2):
        all_of(axis, *kv).wait_send()
        all_of(axis, *queries).wait_send()
    all_of(0, *back).wait_send()
    all_of(1, *back).wait_send()
    all_of(0, *back).wait_recv()
    total = mix(0) + lanes_in(token_refs, slice(None)) + proj_bias[...][None, :]
    all_of(1, *back).wait_recv()
    out_ref[...] = (total + by_row(mix(1))).astype(BF16).reshape(16, 16, DIM)


def on_device(image, conv_weight, conv_bias, merge_gain, merge_shift, norm_gain, norm_shift, qkv_weight, proj_weight, proj_bias):
    dma = pltpu.SemaphoreType.DMA
    return pl.pallas_call(
        kernel,
        out_shape=pltpu.VMEM((16, 16, DIM), BF16),
        in_specs=[pl.BlockSpec(memory_space=pltpu.HBM)] * 10,
        out_specs=pl.BlockSpec(memory_space=pltpu.VMEM),
        scratch_shapes=[pltpu.VMEM((DIM,), F32)] * 6
        + [
            pltpu.VMEM((32, 32, 192), BF16),
            pltpu.VMEM((3, 3, 192, DIM), BF16),
            pltpu.VMEM((DIM, 3 * DIM), BF16),
            pltpu.VMEM((DIM, DIM), BF16),
            pltpu.VMEM((2, 34, 40, 128), F32),
            pltpu.VMEM((3, 17, 2, 16, 192), BF16),
            pltpu.VMEM((3 * DIM, DIM), BF16),
            pltpu.VMEM((80, 128), F32),
            pltpu.VMEM((80, 128), F32),
            pltpu.VMEM((32, 192), BF16),
            pltpu.VMEM((32, 192), BF16),
            pltpu.VMEM((32, 192), BF16),
            pltpu.VMEM((16, 192), BF16),
        ]
        + [pltpu.VMEM((TOKENS, 128), F32)] * 9
        + [pltpu.VMEM((2, PEERS, 2 * DEPTH, 128), BF16)] * 2
        + [pltpu.VMEM((2, PEERS, DEPTH, 128), BF16)] * 4
        + [
            pltpu.VMEM((2, 2048, 128), BF16),
            pltpu.VMEM((2, 32, 2048), BF16),
            pltpu.VMEM((2, 2048, 256), F32),
            dma((10,)),
            dma((3,)),
            dma((3,)),
        ]
        + [dma((2,))] * 6
        + [dma((PEERS // 2,))],
        compiler_params=pltpu.CompilerParams(
            collective_id=0, has_side_effects=True, vmem_limit_bytes=66000000),
    )(image, conv_weight, qkv_weight, proj_weight, conv_bias, merge_gain, merge_shift, norm_gain, norm_shift, proj_bias)


def solution(mesh):
    return jax.shard_map(
        on_device,
        mesh=mesh,
        in_specs=(P("row", "col", None), P(), P(), P(), P(), P(), P(), P(), P(), P()),
        out_specs=P("row", "col", None),
        check_vma=False,
    )
```
